32 devices in a mesh: fsdp: 2 (over x), ctx: 4 (over z), tp: 4 (over y, core).
Axes of the slice: x: 2, y: 2, z: 4, core: 2. Of those that a mesh axis runs over, the one named last changes fastest.
Arguments:
- inputs: bfloat16 [2, 1024, 2048], P('fsdp', 'ctx'), may hold values from -6 to 6
- attn_gain: bfloat16 [2048], P(('fsdp', 'ctx')), may hold values from 0.099609375 to 1.8984375
- qkv_weight: bfloat16 [2048, 3, 2048], P(('fsdp', 'ctx'), None, 'tp'), may hold values from -0.125 to 0.125
- out_weight: bfloat16 [2048, 2048], P(('fsdp', 'ctx'), 'tp'), may hold values from -1 to 1
- qk_gains: bfloat16 [2, 2048], P(None, 'tp'), may hold values from 0.099609375 to 1.8984375
- mlp_gain: bfloat16 [2048], P(('fsdp', 'ctx')), may hold values from 0.099609375 to 1.8984375
- router_weight: bfloat16 [2048, 8], P(('fsdp', 'ctx')), may hold values from -0.0625 to 0.0625
- gate_up_weight: bfloat16 [2048, 2, 8, 1024], P(('fsdp', 'ctx'), None, None, 'tp'), may hold values from -0.125 to 0.125
- down_weight: bfloat16 [2048, 8, 1024], P(('fsdp', 'ctx'), None, 'tp'), may hold values from -1.5 to 1.5
- routes: int32 [4, 2, 256, 4], P('ctx', 'fsdp'), may hold values from 0 to 7, all different within a row; in each aligned block of 256 rows (0 to 255, 256 to 511, ..., all dimensions but the last counted through in order) at most 160 rows name the same one
- cotangent: bfloat16 [2, 1024, 2048], P('fsdp', 'ctx'), may hold values from -6 to 6
Outputs:
- output: bfloat16 [2, 1024, 2048], P('fsdp', 'ctx')
- grad_inputs: float32 [2, 1024, 2048], P('fsdp', 'ctx')
- grad_attn_gain: float32 [2048], P(('fsdp', 'ctx'))
- grad_qkv: float32 [2048, 3, 2048], P(('fsdp', 'ctx'), None, 'tp')
- grad_out: float32 [2048, 2048], P(('fsdp', 'ctx'), 'tp')
- grad_qk_gains: float32 [2, 2048], P(None, 'tp')
- grad_mlp_gain: float32 [2048], P(('fsdp', 'ctx'))
- grad_router: float32 [2048, 8], P(('fsdp', 'ctx'))
- grad_gate_up: float32 [2048, 2, 8, 1024], P(('fsdp', 'ctx'), None, None, 'tp')
- grad_down: float32 [2048, 8, 1024], P(('fsdp', 'ctx'), None, 'tp')
The draws below stay inside these ranges and needn't reach their ends.
Inputs may be any that keep to these rules, and one draw needn't show every extreme that they name: `routes`: each row names 4 different experts. Among the 256 tokens of one device (aligned blocks of the array in its order) no expert is named more than 160 times, a bound that some block reaches.
All inputs are finite; a program needn't handle non-finite values.
Results may differ from the reference program's by a relative error of at most 0.017.
Values may be sent and summed in bfloat16 or wider, within the bound.
A program may use at most 256 MiB of HBM per device.

```python
import math
import jax
import jax.numpy as jnp
import numpy as np
from jax import lax

D = 2048
HEADS = 16
HEAD_DIM = 128
FFN = 1024
TOPK = 4
EXPERTS = 8
BLK = 256
SEQ_DEV = 1
HQ = 2048
SEQS = 2
LEN = 1024
CAP = 160
N_FSDP = 2
N_CTX = 4


def steps_of(stream_key, shape, shards, low, top_value):
    def one(position, blocks):
        heights = jax.random.uniform(jax.random.fold_in(jax.random.fold_in(stream_key, 6), position), (blocks,), jnp.float32, low / len(shards), top_value / len(shards))
        return jnp.repeat(jnp.exp(heights), shape[position] // blocks).reshape((-1,) + (1,) * (len(shape) - position - 1))

    gain = one(*shards[0])
    for cut in shards[1:]:
        gain = gain * one(*cut)
    return gain


def assign_block(stream_key, own, number, rows, number_of, top, bound, lean):
    sequence = jax.random.permutation(stream_key, number_of)
    heavy_load, usual = load_shares(number_of, rows * top, bound, lean, True), load_shares(number_of, rows * top, bound, lean, False)
    places = jnp.arange(number_of)

    def named(lengths, offset_by):
        used = int((lengths > 0).sum())
        fixed = max(1, used // 4)
        shifted = fixed + (places - fixed + offset_by * (used - fixed)) % max(1, number_of - fixed)
        return jnp.zeros((number_of,), jnp.int32).at[sequence[jnp.where(places < fixed, places, shifted)]].set(jnp.asarray(lengths, jnp.int32))

    lengths = jnp.where(number % 4 == 0, named(heavy_load, number // 4), named(usual, number - number // 4 - 1))
    mixed = jax.random.permutation(jax.random.fold_in(own, 3), number_of)
    giver, receiver = mixed[0:number_of // 2 * 2:2], mixed[1:number_of // 2 * 2:2]
    slack = jnp.minimum(lengths[giver] - 1, bound - lengths[receiver]) // 2
    slack = jnp.where((giver == sequence[0]) | (receiver == sequence[0]) | (lengths[receiver] == 0), 0, jnp.maximum(slack, 0))
    shifted = jax.random.randint(jax.random.fold_in(own, 4), (number_of // 2,), 0, 1 << 20) % (slack + 1)
    lengths = lengths.at[giver].add(-shifted).at[receiver].add(shifted)
    members = jnp.searchsorted(jnp.cumsum(lengths), jnp.arange(rows * top), side="right").astype(jnp.int32)
    table = members.reshape(top, rows).T
    table = table[jax.random.permutation(jax.random.fold_in(own, 1), rows)]
    offset_by = jax.random.randint(jax.random.fold_in(own, 2), (rows, 1), 0, top)
    return jnp.take_along_axis(table, (jnp.arange(top)[None, :] + offset_by) % top, axis=1)


def load_shares(amount, total, bound, lean, full):
    loads = [(1 << 20) // math.isqrt(grade ** lean) + 1 for grade in range(1, amount + 1)]
    largest = bound if full else min(bound, max(-(-total // amount), total * loads[0] // sum(loads)))
    least = 1 if total - largest >= amount - 1 else 0
    holding, surplus = [largest] + [least] * (amount - 1), total - largest - least * (amount - 1)
    while surplus > 0:
        candidates = [i for i in range(1, amount) if holding[i] < largest] or [i for i in range(1, amount) if holding[i] < bound]
        whole, budget = sum([loads[i] for i in candidates]), surplus
        for i in candidates:
            extra = min(bound - holding[i], max(1, budget * loads[i] // whole), surplus)
            holding[i] = holding[i] + extra
            surplus = surplus - extra
    return np.array(holding)


def scatter_about(key, extent, scale, limit, split=(), kind=jnp.bfloat16):
    entries = scale * jax.random.normal(key, extent, jnp.float32)
    if split:
        entries = entries * steps_of(key, extent, split, -0.22, 0.18)
    return jnp.clip(entries, -limit, limit).astype(kind)


def setup_inputs(seed: int = 0) -> dict:
    streams_of = jax.random.split(jax.random.key(seed), 12)
    inputs = scatter_about(streams_of[0], (SEQS, LEN, D), 1.0, 6.0, ((0, 2), (1, 4)))
    attn_gain = jnp.clip(1.0 + 0.18 * jax.random.normal(streams_of[1], (D,), jnp.float32), 0.099609375, 1.8984375).astype(jnp.bfloat16)
    qkv_weight = scatter_about(streams_of[2], (D, 3, HQ), D ** -0.5, 0.125, ((0, 8), (2, 4)))
    out_weight = scatter_about(streams_of[3], (D, HQ), (max(HQ // 64, 1)) ** -0.5, 1.0, ((0, 8), (1, 4)))
    qk_gains = jnp.clip(1.0 + 0.18 * jax.random.normal(streams_of[4], (2, HQ), jnp.float32), 0.099609375, 1.8984375).astype(jnp.bfloat16)
    mlp_gain = jnp.clip(1.0 + 0.18 * jax.random.normal(streams_of[5], (D,), jnp.float32), 0.099609375, 1.8984375).astype(jnp.bfloat16)
    router_weight = scatter_about(streams_of[6], (D, EXPERTS), (4 * D) ** -0.5, 0.0625, ((0, 8),))
    gate_up_weight = scatter_about(streams_of[7], (D, 2, EXPERTS, FFN), D ** -0.5, 0.125, ((0, 8), (3, 4)))
    down_weight = scatter_about(streams_of[8], (D, EXPERTS, FFN), (max(FFN // 64, 1)) ** -0.5, 1.5, ((0, 8), (2, 4)))
    routes_keys = jax.random.split(jax.random.fold_in(streams_of[9], 1), N_CTX * SEQS * BLK // (SEQ_DEV * BLK))
    routes_turns = jax.random.permutation(jax.random.fold_in(streams_of[9], 3), N_CTX * SEQS * BLK // (SEQ_DEV * BLK))
    routes = jax.vmap(lambda own, number: assign_block(jax.random.fold_in(streams_of[9], 2), own, number, SEQ_DEV * BLK, EXPERTS, TOPK, CAP, 1))(routes_keys, routes_turns).reshape((N_CTX, SEQS, BLK, TOPK))
    cotangent = scatter_about(streams_of[10], (SEQS, LEN, D), 1.0, 6.0, ((0, 2), (1, 4)))
    return {"inputs": inputs, "attn_gain": attn_gain, "qkv_weight": qkv_weight, "out_weight": out_weight, "qk_gains": qk_gains, "mlp_gain": mlp_gain, "router_weight": router_weight, "gate_up_weight": gate_up_weight, "down_weight": down_weight, "routes": routes, "cotangent": cotangent}


@jax.custom_vjp
def low(v):
    return lax.optimization_barrier(v.astype(jnp.bfloat16)).astype(jnp.float32)

@jax.custom_vjp
def low_back(v):
    return v

def low_keep(v):
    return (low(v), None)

def low_pass(kept, grad):
    return (grad,)

def back_keep(v):
    return (v, None)

def back_low(kept, grad):
    return (low(grad),)
low.defvjp(low_keep, low_pass)
low_back.defvjp(back_keep, back_low)
epsilon = 1e-05
highest = lax.Precision.HIGHEST

def inv_rms(values):
    return lax.rsqrt(lax.optimization_barrier(jnp.mean(values * values, axis=-1, keepdims=True)) + epsilon)

def rotary_tables(offset, length):
    half_dim = HEAD_DIM // 2
    frequency = jnp.exp(jnp.arange(half_dim, dtype=jnp.float32) * (-2.0 * math.log(10000.0) / HEAD_DIM))
    positions = (offset + jnp.arange(length, dtype=jnp.int32)).astype(jnp.float32)
    angles = positions[:, None] * frequency[None, :]
    angles = jnp.concatenate([angles, angles], axis=1)
    return (jnp.cos(angles), jnp.sin(angles))

def rotate(values, cosine, sine_table):
    half_dim = values.shape[-1] // 2
    turned = jnp.concatenate([-values[..., half_dim:], values[..., :half_dim]], axis=-1)
    return values * cosine + turned * sine_table

def slot_table(routed):
    flat_routes = routed.reshape(-1)
    one_hot = (flat_routes[:, None] == jnp.arange(EXPERTS, dtype=jnp.int32)[None, :]).astype(jnp.int32)
    earlier = jnp.cumsum(one_hot, axis=0) - one_hot
    within = lax.optimization_barrier(jnp.sum(earlier * one_hot, axis=1))
    slots = flat_routes * CAP + within
    owners = jnp.arange(flat_routes.shape[0], dtype=jnp.int32) // TOPK
    token_of = jnp.zeros((EXPERTS * CAP,), jnp.int32).at[slots].set(owners)
    filled = jnp.zeros((EXPERTS * CAP,), jnp.float32).at[slots].set(1.0)
    return (slots.reshape(routed.shape), token_of, filled)

def attend_group(seq_group, attn_gain, qkv_weight, out_weight, qk_gains, cosine, sine_table):
    groups, length = (seq_group.shape[0], seq_group.shape[1])
    normed = low(seq_group * inv_rms(seq_group) * attn_gain)
    projected = jnp.einsum('gtd,dch->gtch', normed, qkv_weight, precision=highest)
    query_proj = low_back(projected[:, :, 0])
    key_proj = low_back(projected[:, :, 1])
    value_proj = low(low_back(projected[:, :, 2]))
    query_norm = query_proj * inv_rms(query_proj) * qk_gains[0]
    key_norm = key_proj * inv_rms(key_proj) * qk_gains[1]
    head_shape = (groups, length, HEADS, HEAD_DIM)
    query_rot = low(rotate(query_norm.reshape(head_shape), cosine[:, None, :], sine_table[:, None, :]))
    key_rot = low(rotate(key_norm.reshape(head_shape), cosine[:, None, :], sine_table[:, None, :]))
    value_heads = value_proj.reshape(head_shape)
    scores = low_back(jnp.einsum('gqhd,gkhd->ghqk', query_rot, key_rot, precision=highest) * (1.0 / math.sqrt(HEAD_DIM)))
    block_of = jnp.arange(length, dtype=jnp.int32) // BLK
    allowed = block_of[None, :] <= block_of[:, None]
    scores = jnp.where(allowed[None, None], scores, -1e+30)
    softmaxed = jax.nn.softmax(scores, axis=-1)
    mixed = jnp.einsum('ghqk,gkhd->gqhd', low(softmaxed), value_heads, precision=highest)
    attended = low(low_back(mixed.reshape(groups, length, HQ)))
    branch = low_back(jnp.einsum('gth,dh->gtd', attended, out_weight, precision=highest))
    return seq_group + branch

def expert_block(block_inputs, gate_up_weight, down_weight):
    normed_rows, gate_rows, routed = block_inputs
    slots, token_of, filled = slot_table(routed)
    dispatched = (normed_rows[token_of] * filled[:, None]).reshape(EXPERTS, CAP, D)
    gate_up = low_back(jnp.einsum('ecd,djef->ecjf', dispatched, gate_up_weight, precision=highest))
    activated = low(jax.nn.silu(gate_up[:, :, 0]) * gate_up[:, :, 1])
    returned = low_back(jnp.einsum('ecf,def->ecd', activated, down_weight, precision=highest)).reshape(EXPERTS * CAP, D)
    return lax.optimization_barrier(jnp.sum(gate_rows[:, :, None] * returned[slots], axis=1))

def to_blocks(values):
    width = values.shape[-1]
    shaped = values.reshape(N_FSDP, SEQ_DEV, N_CTX, BLK, width).transpose(2, 0, 1, 3, 4)
    return shaped.reshape(N_CTX * N_FSDP, SEQ_DEV * BLK, width)

def from_blocks(values):
    shaped = values.reshape(N_CTX, N_FSDP, SEQ_DEV, BLK, D).transpose(1, 2, 0, 3, 4)
    return shaped.reshape(SEQS, LEN, D)

def forward(inputs, attn_gain, qkv_weight, out_weight, qk_gains, mlp_gain, router_weight, gate_up_weight, down_weight, routes):
    per_group = math.gcd(SEQS, 4)
    cosine, sine_table = rotary_tables(0, LEN)
    grouped = inputs.reshape(SEQS // per_group, per_group, LEN, D)

    def attend(seq_group):
        return attend_group(seq_group, attn_gain, qkv_weight, out_weight, qk_gains, cosine, sine_table)
    middle = lax.map(jax.checkpoint(attend), grouped).reshape(SEQS, LEN, D)
    normed_mlp = low(middle * inv_rms(middle) * mlp_gain)
    logits = jnp.einsum('std,de->ste', normed_mlp, router_weight, precision=highest)
    chances = jax.nn.softmax(logits, axis=-1)
    routed = routes.reshape(N_CTX * N_FSDP, SEQ_DEV * BLK, TOPK)
    gates = jnp.take_along_axis(to_blocks(chances), routed, axis=-1)

    def experts_of(block_inputs):
        return expert_block(block_inputs, gate_up_weight, down_weight)
    added = lax.map(jax.checkpoint(experts_of), (to_blocks(normed_mlp), gates, routed))
    return middle + from_blocks(added)

def reference(inputs, attn_gain, qkv_weight, out_weight, qk_gains, mlp_gain, router_weight, gate_up_weight, down_weight, routes, cotangent):
    params = [value.astype(jnp.float32) for value in (inputs, attn_gain, qkv_weight, out_weight, qk_gains, mlp_gain, router_weight, gate_up_weight, down_weight)]

    def layer(*weights):
        return forward(*weights, routes)
    result, pullback = jax.vjp(layer, *params)
    grads = pullback(cotangent.astype(jnp.float32))
    return (result.astype(jnp.bfloat16), grads[0], grads[1], grads[2], grads[3], grads[4], grads[5], grads[6], grads[7], grads[8])
```

```python
import math

import jax
import jax.numpy as jnp
from jax import lax
from jax.sharding import PartitionSpec as P

HEAD_DIM = 128
TOPK = 4
EXPERTS = 8
HQ = 2048
CAP = 160


epsilon = 1e-05
highest = lax.Precision.HIGHEST


def inv_rms(values):
    return lax.rsqrt(jnp.mean(values * values, axis=-1, keepdims=True) + epsilon)


def rotary_tables(offset, length):
    half_dim = HEAD_DIM // 2
    frequency = jnp.exp(
        jnp.arange(half_dim, dtype=jnp.float32) * (-2.0 * math.log(10000.0) / HEAD_DIM)
    )
    positions = (offset + jnp.arange(length, dtype=jnp.int32)).astype(jnp.float32)
    angles = positions[:, None] * frequency[None, :]
    angles = jnp.concatenate([angles, angles], axis=1)
    return (jnp.cos(angles), jnp.sin(angles))


def rotate(values, cosine, sine_table):
    half_dim = values.shape[-1] // 2
    turned = jnp.concatenate([-values[..., half_dim:], values[..., :half_dim]], axis=-1)
    return values * cosine + turned * sine_table


def rotate_back(grads, cosine, sine_table):
    half_dim = grads.shape[-1] // 2
    scaled = grads * sine_table
    return grads * cosine + jnp.concatenate(
        [scaled[..., half_dim:], -scaled[..., :half_dim]], axis=-1
    )


def slot_table(routed):
    flat_routes = routed.reshape(-1)
    one_hot = (flat_routes[:, None] == jnp.arange(EXPERTS, dtype=jnp.int32)[None, :]).astype(
        jnp.int32
    )
    earlier = jnp.cumsum(one_hot, axis=0) - one_hot
    within = jnp.sum(earlier * one_hot, axis=1)
    slots = flat_routes * CAP + within
    owners = jnp.arange(flat_routes.shape[0], dtype=jnp.int32) // TOPK
    token_of = jnp.zeros((EXPERTS * CAP,), jnp.int32).at[slots].set(owners)
    filled = jnp.zeros((EXPERTS * CAP,), jnp.float32).at[slots].set(1.0)
    return (slots.reshape(routed.shape), token_of, filled)


def on_device(
    inputs,
    attn_gain,
    qkv_weight,
    out_weight,
    qk_gains,
    mlp_gain,
    router_weight,
    gate_up_weight,
    down_weight,
    routes,
    cotangent,
):
    seq_dev, block, width = inputs.shape
    rows = seq_dev * block
    heads_dev = qkv_weight.shape[2] // HEAD_DIM
    scale = 1.0 / math.sqrt(HEAD_DIM)
    place = lax.axis_index("ctx")
    attn_gain_all, qkv_all, out_all, mlp_gain_all, router_all = (
        lax.all_gather(attn_gain, ("fsdp", "ctx"), axis=0, tiled=True),
        lax.all_gather(qkv_weight, ("fsdp", "ctx"), axis=0, tiled=True),
        lax.all_gather(out_weight, ("fsdp", "ctx"), axis=0, tiled=True),
        lax.all_gather(mlp_gain, ("fsdp", "ctx"), axis=0, tiled=True),
        lax.all_gather(router_weight, ("fsdp", "ctx"), axis=0, tiled=True),
    )
    attn_scale = attn_gain_all.astype(jnp.float32)
    mlp_scale = mlp_gain_all.astype(jnp.float32)
    flat_in = inputs.reshape(rows, width).astype(jnp.float32)
    first_rms = inv_rms(flat_in)
    normed = (flat_in * first_rms * attn_scale).astype(jnp.bfloat16)
    projected = jnp.einsum("td,dch->tch", normed, qkv_all, preferred_element_type=jnp.float32)
    query_proj = projected[:, 0]
    key_proj = projected[:, 1]
    query_sums, key_sums = lax.psum(
        (jnp.sum(query_proj * query_proj, axis=-1), jnp.sum(key_proj * key_proj, axis=-1)), "tp"
    )
    query_rms = lax.rsqrt(query_sums / HQ + epsilon)[:, None]
    key_rms = lax.rsqrt(key_sums / HQ + epsilon)[:, None]
    query_gain = qk_gains[0].astype(jnp.float32)
    key_gain = qk_gains[1].astype(jnp.float32)
    query_norm = query_proj * query_rms * query_gain
    key_norm = key_proj * key_rms * key_gain
    cosine, sine_table = rotary_tables(place * block, block)
    cos_heads = cosine[:, None, :]
    sin_heads = sine_table[:, None, :]
    head_shape = (seq_dev, block, heads_dev, HEAD_DIM)
    query_rot = rotate(query_norm.reshape(head_shape), cos_heads, sin_heads).astype(jnp.bfloat16)
    key_rot = rotate(key_norm.reshape(head_shape), cos_heads, sin_heads).astype(jnp.bfloat16)
    value_heads = projected[:, 2].reshape(head_shape).astype(jnp.bfloat16)
    key_all, value_all = (
        lax.all_gather(key_rot, "ctx", axis=1, tiled=True),
        lax.all_gather(value_heads, "ctx", axis=1, tiled=True),
    )
    length = key_all.shape[1]
    key_block = jnp.arange(length, dtype=jnp.int32) // block
    allowed = (key_block <= place)[None, None, None, :]
    scores = (
        jnp.einsum("sqhd,skhd->shqk", query_rot, key_all, preferred_element_type=jnp.float32)
        * scale
    )
    scores = jnp.where(allowed, scores, -1e30)
    top_score = jnp.max(scores, axis=-1, keepdims=True)
    exponent = jnp.exp(scores - top_score)
    total = jnp.sum(exponent, axis=-1, keepdims=True)
    log_total = top_score + jnp.log(total)
    softmaxed = exponent / total
    attended = jnp.einsum(
        "shqk,skhd->sqhd",
        softmaxed.astype(jnp.bfloat16),
        value_all,
        preferred_element_type=jnp.float32,
    )
    attended = attended.reshape(rows, heads_dev * HEAD_DIM).astype(jnp.bfloat16)
    branch = lax.psum(
        jnp.einsum("th,dh->td", attended, out_all, preferred_element_type=jnp.float32), "tp"
    )
    middle = flat_in + branch
    second_rms = inv_rms(middle)
    normed_mlp = (middle * second_rms * mlp_scale).astype(jnp.bfloat16)
    logits = jnp.dot(normed_mlp, router_all, preferred_element_type=jnp.float32)
    chances = jax.nn.softmax(logits, axis=-1)
    routed = routes.reshape(rows, TOPK)
    gates = jnp.take_along_axis(chances, routed, axis=-1)
    slots, token_of, filled = slot_table(routed)
    dispatched = (normed_mlp[token_of] * filled[:, None].astype(jnp.bfloat16)).reshape(
        EXPERTS, CAP, width
    )
    gate_up_all, down_all = (
        lax.all_gather(gate_up_weight, ("fsdp", "ctx"), axis=0, tiled=True),
        lax.all_gather(down_weight, ("fsdp", "ctx"), axis=0, tiled=True),
    )
    gate_up = jnp.einsum(
        "ecd,djef->ecjf", dispatched, gate_up_all, preferred_element_type=jnp.float32
    )
    gate_part = gate_up[:, :, 0]
    up_part = gate_up[:, :, 1]
    activated = (jax.nn.silu(gate_part) * up_part).astype(jnp.bfloat16)
    upstream = cotangent.reshape(rows, width).astype(jnp.float32)
    slot_gates = (
        jnp.zeros((EXPERTS * CAP,), jnp.float32)
        .at[slots.reshape(-1)]
        .set(gates.reshape(-1))
        .reshape(EXPERTS, CAP)
    )
    token_grid = token_of.reshape(EXPERTS, CAP)
    filled_grid = filled.reshape(EXPERTS, CAP)

    def expert_forward(expert_index, running):
        combined, slot_products = running
        expert_down = lax.dynamic_index_in_dim(down_all, expert_index, 1, keepdims=False)
        expert_act = lax.dynamic_index_in_dim(activated, expert_index, 0, keepdims=False)
        expert_tokens = lax.dynamic_index_in_dim(token_grid, expert_index, 0, keepdims=False)
        expert_gates = lax.dynamic_index_in_dim(slot_gates, expert_index, 0, keepdims=False)
        returned_rows = jnp.einsum(
            "cf,df->cd", expert_act, expert_down, preferred_element_type=jnp.float32
        )
        combined = combined.at[expert_tokens].add(returned_rows * expert_gates[:, None])
        products = jnp.sum(returned_rows * upstream[expert_tokens], axis=-1)
        slot_products = lax.dynamic_update_index_in_dim(slot_products, products, expert_index, 0)
        return (combined, slot_products)

    combined, slot_products = lax.fori_loop(
        0,
        EXPERTS,
        expert_forward,
        (jnp.zeros((rows, width), jnp.float32), jnp.zeros((EXPERTS, CAP), jnp.float32)),
    )
    gate_grad_part = slot_products.reshape(-1)[slots]
    expert_sum = lax.psum(combined, "tp")
    output = (middle + expert_sum).astype(jnp.bfloat16).reshape(seq_dev, block, width)
    slot_grads = (
        (slot_gates.reshape(-1)[:, None] * upstream[token_of])
        .astype(jnp.bfloat16)
        .reshape(EXPERTS, CAP, width)
    )
    gate_up_back, down_back = (
        lax.all_gather(gate_up_weight, ("fsdp", "ctx"), axis=0, tiled=True),
        lax.all_gather(down_weight, ("fsdp", "ctx"), axis=0, tiled=True),
    )
    act_grads = jnp.einsum(
        "ecd,def->ecf", slot_grads, down_back, preferred_element_type=jnp.float32
    )
    sigmoid = jax.nn.sigmoid(gate_part)
    gate_grads = act_grads * up_part * sigmoid * (1.0 + gate_part * (1.0 - sigmoid))
    up_grads = act_grads * (gate_part * sigmoid)
    pre_grads = jnp.stack([gate_grads, up_grads], axis=2).astype(jnp.bfloat16)

    def expert_backward(expert_index, running):
        expert_pre = lax.dynamic_index_in_dim(pre_grads, expert_index, 0, keepdims=False)
        expert_weight = lax.dynamic_index_in_dim(gate_up_back, expert_index, 2, keepdims=False)
        expert_tokens = lax.dynamic_index_in_dim(token_grid, expert_index, 0, keepdims=False)
        expert_filled = lax.dynamic_index_in_dim(filled_grid, expert_index, 0, keepdims=False)
        expert_back = jnp.einsum(
            "cjf,djf->cd", expert_pre, expert_weight, preferred_element_type=jnp.float32
        )
        return running.at[expert_tokens].add(expert_back * expert_filled[:, None])

    expert_input_part = lax.fori_loop(
        0, EXPERTS, expert_backward, jnp.zeros((rows, width), jnp.float32)
    )
    gate_up_term = jnp.einsum(
        "ecd,ecjf->djef", dispatched, pre_grads, preferred_element_type=jnp.float32
    )
    down_term = jnp.einsum(
        "ecf,ecd->def", activated, slot_grads, preferred_element_type=jnp.float32
    )
    expert_grads = lax.psum_scatter(
        jnp.concatenate([gate_up_term, down_term[:, None]], axis=1),
        ("fsdp", "ctx"),
        scatter_dimension=0,
        tiled=True,
    )
    gate_up_share = expert_grads[:, :2]
    down_share = expert_grads[:, 2]
    expert_input, gate_total = lax.psum((expert_input_part, gate_grad_part), "tp")
    chosen = (routed[:, :, None] == jnp.arange(EXPERTS, dtype=jnp.int32)[None, None, :]).astype(
        jnp.float32
    )
    chance_grads = jnp.sum(gate_total[:, :, None] * chosen, axis=1)
    logit_grads = chances * (chance_grads - jnp.sum(chances * chance_grads, axis=-1, keepdims=True))
    router_f32 = router_all.astype(jnp.float32)
    mlp_input = expert_input + jnp.dot(logit_grads, router_f32.T, precision=highest)
    grad_router = jnp.dot(normed_mlp.astype(jnp.float32).T, logit_grads, precision=highest)
    grad_mlp_gain = jnp.sum(mlp_input * middle * second_rms, axis=0)
    scaled_mlp = mlp_input * mlp_scale
    middle_grad = (
        upstream
        + second_rms * scaled_mlp
        - middle * second_rms**3 / width * jnp.sum(scaled_mlp * middle, axis=-1, keepdims=True)
    )
    branch_grad = middle_grad.astype(jnp.bfloat16)
    grad_out = jnp.einsum("td,th->dh", branch_grad, attended, preferred_element_type=jnp.float32)
    attended_grad = (
        jnp.dot(branch_grad, out_all, preferred_element_type=jnp.float32)
        .astype(jnp.bfloat16)
        .reshape(head_shape)
    )
    again_scores = (
        jnp.einsum("sqhd,skhd->shqk", query_rot, key_all, preferred_element_type=jnp.float32)
        * scale
    )
    again_scores = jnp.where(allowed, again_scores, -1e30)
    recomputed = jnp.exp(again_scores - log_total)
    prob_grads = jnp.einsum(
        "sqhd,skhd->shqk", attended_grad, value_all, preferred_element_type=jnp.float32
    )
    score_grads = (
        recomputed * (prob_grads - jnp.sum(recomputed * prob_grads, axis=-1, keepdims=True))
    ).astype(jnp.bfloat16)
    query_grads = (
        jnp.einsum("shqk,skhd->sqhd", score_grads, key_all, preferred_element_type=jnp.float32)
        * scale
    )
    key_grads = (
        jnp.einsum("shqk,sqhd->skhd", score_grads, query_rot, preferred_element_type=jnp.float32)
        * scale
    )
    value_grads = jnp.einsum(
        "shqk,sqhd->skhd",
        recomputed.astype(jnp.bfloat16),
        attended_grad,
        preferred_element_type=jnp.float32,
    )
    key_back, value_back = (
        lax.psum_scatter(key_grads, "ctx", scatter_dimension=1, tiled=True),
        lax.psum_scatter(value_grads, "ctx", scatter_dimension=1, tiled=True),
    )
    query_norm_grad = rotate_back(query_grads, cos_heads, sin_heads).reshape(rows, -1)
    key_norm_grad = rotate_back(key_back, cos_heads, sin_heads).reshape(rows, -1)
    query_scaled = query_norm_grad * query_gain
    key_scaled = key_norm_grad * key_gain
    query_inner, key_inner = lax.psum(
        (jnp.sum(query_scaled * query_proj, axis=-1), jnp.sum(key_scaled * key_proj, axis=-1)), "tp"
    )
    query_pre = query_rms * query_scaled - query_proj * query_rms**3 / HQ * query_inner[:, None]
    key_pre = key_rms * key_scaled - key_proj * key_rms**3 / HQ * key_inner[:, None]
    gain_terms = jnp.stack(
        [
            jnp.sum(query_norm_grad * query_proj * query_rms, axis=0),
            jnp.sum(key_norm_grad * key_proj * key_rms, axis=0),
        ]
    )
    grad_qk_gains = lax.psum(gain_terms, ("fsdp", "ctx"))
    proj_grads = jnp.stack([query_pre, key_pre, value_back.reshape(rows, -1)], axis=1).astype(
        jnp.bfloat16
    )
    grad_qkv = jnp.einsum("td,tch->dch", normed, proj_grads, preferred_element_type=jnp.float32)
    normed_grad = lax.psum(
        jnp.einsum("tch,dch->td", proj_grads, qkv_all, preferred_element_type=jnp.float32), "tp"
    )
    grad_attn_gain = jnp.sum(normed_grad * flat_in * first_rms, axis=0)
    scaled_first = normed_grad * attn_scale
    grad_inputs = (
        middle_grad
        + first_rms * scaled_first
        - flat_in * first_rms**3 / width * jnp.sum(scaled_first * flat_in, axis=-1, keepdims=True)
    )
    shares = (
        lax.psum_scatter(grad_attn_gain, ("fsdp", "ctx"), scatter_dimension=0, tiled=True),
        lax.psum_scatter(grad_qkv, ("fsdp", "ctx"), scatter_dimension=0, tiled=True),
        lax.psum_scatter(grad_out, ("fsdp", "ctx"), scatter_dimension=0, tiled=True),
        lax.psum_scatter(grad_mlp_gain, ("fsdp", "ctx"), scatter_dimension=0, tiled=True),
        lax.psum_scatter(grad_router, ("fsdp", "ctx"), scatter_dimension=0, tiled=True),
    )
    return (
        output,
        grad_inputs.reshape(seq_dev, block, width),
        shares[0],
        shares[1],
        shares[2],
        grad_qk_gains,
        shares[3],
        shares[4],
        gate_up_share,
        down_share,
    )


def attend_scores(query_rot, key_rot, scale, block):
    scores = jnp.einsum("qd,kd->qk", query_rot, key_rot, preferred_element_type=jnp.float32) * scale
    length = scores.shape[0]
    place = jnp.arange(length, dtype=jnp.int32) // block
    return jnp.where(place[None, :] <= place[:, None], scores, -1e30)


def by_head(
    sizes,
    inputs,
    attn_gain,
    qkv_weight,
    out_weight,
    qk_gains,
    mlp_gain,
    router_weight,
    gate_up_weight,
    down_weight,
    routes,
    cotangent,
):
    n_fsdp, n_ctx, n_tp = sizes
    places = n_fsdp * n_ctx
    both = ("fsdp", "ctx")
    f32, bf16 = jnp.float32, jnp.bfloat16
    _, block, width = inputs.shape
    depth = width // places
    quarter = width // n_tp
    length = n_ctx * block
    hidden = gate_up_weight.shape[3]
    scale = 1.0 / math.sqrt(HEAD_DIM)
    ctx, tp = lax.axis_index("ctx"), lax.axis_index("tp")

    def own_quarter(values):
        return lax.dynamic_slice_in_dim(values, tp * quarter, quarter, axis=1)

    attn_scale = attn_gain.astype(f32)
    mlp_scale = mlp_gain.astype(f32)
    qkv_raw = qkv_weight.reshape(depth, 3, n_ctx, HEAD_DIM).transpose(2, 0, 1, 3)
    qkv_raw = qkv_raw.reshape(n_ctx, depth, 3 * HEAD_DIM).astype(f32)
    qkv_scaled = (qkv_raw * attn_scale[None, :, None]).astype(bf16)
    head_weight = lax.all_to_all(qkv_scaled, "ctx", 0, 0, tiled=True)
    head_weight = lax.all_gather(head_weight, "fsdp", axis=0, tiled=True)
    head_weight = head_weight.reshape(width, 3 * HEAD_DIM)
    gate_up_raw = gate_up_weight.transpose(2, 0, 1, 3).reshape(EXPERTS, depth, 2 * hidden)
    down_raw = down_weight.transpose(1, 0, 2)
    expert_send = jnp.concatenate(
        [(gate_up_raw.astype(f32) * mlp_scale[None, :, None]).astype(bf16), down_raw], axis=2
    )
    expert_weight = lax.all_to_all(expert_send, both, 0, 0, tiled=True)
    expert_weight = expert_weight.reshape(width, 3 * hidden)
    gate_up_full = expert_weight[:, : 2 * hidden]
    down_full = expert_weight[:, 2 * hidden :]
    out_all = lax.all_gather(out_weight, both, axis=0, tiled=True)
    router_f32 = router_weight.astype(f32)
    router_all = lax.all_gather(router_f32 * mlp_scale[:, None], both, axis=0, tiled=True)
    router_part = lax.dynamic_slice_in_dim(router_all, tp * quarter, quarter, axis=0)

    routed = routes.reshape(block, TOPK)
    named = (routed[:, :, None] == jnp.arange(EXPERTS, dtype=jnp.int32)).astype(f32).sum(axis=1)
    order = jnp.arange(block, dtype=jnp.int32)
    before = (order[None, :] < order[:, None]).astype(bf16)
    earlier = jnp.dot(before, named.astype(bf16), preferred_element_type=f32).astype(jnp.int32)
    slot_of = jnp.where(named > 0, earlier, -1)
    picks = slot_of.T[:, None, :] == jnp.arange(CAP, dtype=jnp.int32)[None, :, None]
    pick_f32 = picks.astype(f32)
    pick = picks.astype(bf16).reshape(EXPERTS * CAP, block)

    def dispatch(part):
        rows = jnp.dot(pick, part, preferred_element_type=f32).astype(bf16)
        rows = lax.all_to_all(rows.reshape(EXPERTS, CAP, quarter), both, 0, 0, tiled=True)
        rows = lax.all_gather(rows, "tp", axis=2, tiled=True)
        return rows.reshape(EXPERTS * CAP, width)

    def bring_back(rows):
        rows = lax.psum_scatter(
            rows.reshape(EXPERTS, CAP, width), "tp", scatter_dimension=2, tiled=True
        )
        rows = lax.all_to_all(rows, both, 0, 0, tiled=True).reshape(EXPERTS * CAP, quarter)
        return lax.dot_general(pick, rows, (((0,), (0,)), ((), ())), preferred_element_type=f32)

    upstream_part = own_quarter(cotangent.reshape(block, width))
    up_rows = dispatch(upstream_part)
    upstream_part = upstream_part.astype(f32)

    flat_in = inputs.reshape(block, width).astype(f32)
    first_rms = inv_rms(flat_in)
    in_part = own_quarter(flat_in)
    normed_own = (flat_in * first_rms).astype(bf16)
    share = block // n_tp
    normed_share = lax.dynamic_slice_in_dim(normed_own, tp * share, share, axis=0)
    normed = lax.all_gather(normed_share, ("ctx", "tp"), axis=0, tiled=True)
    projected = jnp.dot(normed, head_weight, preferred_element_type=f32)
    query_proj = projected[:, :HEAD_DIM]
    key_proj = projected[:, HEAD_DIM : 2 * HEAD_DIM]
    value_heads = projected[:, 2 * HEAD_DIM :].astype(bf16)
    sums = lax.psum(
        jnp.stack([jnp.sum(query_proj * query_proj, axis=-1), jnp.sum(key_proj * key_proj, axis=-1)]),
        ("ctx", "tp"),
    )
    query_rms = lax.rsqrt(sums[0] / HQ + epsilon)[:, None]
    key_rms = lax.rsqrt(sums[1] / HQ + epsilon)[:, None]
    own_gains = lax.dynamic_slice_in_dim(qk_gains, ctx * HEAD_DIM, HEAD_DIM, axis=1).astype(f32)
    query_gain, key_gain = own_gains[0], own_gains[1]
    cosine, sine_table = rotary_tables(0, length)
    query_rot = rotate(query_proj * query_rms * query_gain, cosine, sine_table).astype(bf16)
    key_rot = rotate(key_proj * key_rms * key_gain, cosine, sine_table).astype(bf16)
    scores = attend_scores(query_rot, key_rot, scale, block)
    exponent = jnp.exp(scores - jnp.max(scores, axis=-1, keepdims=True))
    probs = exponent / jnp.sum(exponent, axis=-1, keepdims=True)
    probs_low = probs.astype(bf16)
    attended = jnp.dot(probs_low, value_heads, preferred_element_type=f32).astype(bf16)
    attended = lax.all_to_all(attended.reshape(n_ctx, block, HEAD_DIM), "ctx", 0, 0, tiled=True)
    attended = attended.transpose(1, 0, 2).reshape(block, n_ctx * HEAD_DIM)
    branch = jnp.einsum("th,dh->td", attended, out_all, preferred_element_type=f32)
    branch = lax.psum_scatter(branch.astype(bf16), "tp", scatter_dimension=1, tiled=True)
    middle = in_part + branch.astype(f32)

    small = jnp.concatenate(
        [
            jnp.dot(middle, router_part, precision=highest),
            jnp.sum(middle * middle, axis=-1, keepdims=True),
        ],
        axis=1,
    )
    small = lax.psum(small, "tp")
    raw_logits = small[:, :EXPERTS]
    second_rms = lax.rsqrt(small[:, EXPERTS:] / width + epsilon)
    chances = jax.nn.softmax(raw_logits * second_rms, axis=-1)
    normed_mlp = (middle * second_rms).astype(bf16)
    rows = dispatch(normed_mlp)
    slot_gates = jnp.sum(pick_f32 * chances.T[:, None, :], axis=-1)
    slot_gates = lax.all_to_all(slot_gates, both, 0, 0, tiled=True).reshape(EXPERTS * CAP, 1)

    gate_up = jnp.dot(rows, gate_up_full, preferred_element_type=f32)
    gate_part, up_part = gate_up[:, :hidden], gate_up[:, hidden:]
    sigmoid = jax.nn.sigmoid(gate_part)
    silu = gate_part * sigmoid
    activated = silu * up_part
    act_low = (activated * slot_gates).astype(bf16)
    act_grads = jnp.dot(up_rows, down_full, preferred_element_type=f32)
    slot_products = jnp.sum(activated * act_grads, axis=-1)
    gated = act_grads * slot_gates
    pre_grads = jnp.concatenate(
        [gated * up_part * sigmoid * (1.0 + gate_part * (1.0 - sigmoid)), gated * silu], axis=1
    ).astype(bf16)
    back_rows = lax.dot_general(
        pre_grads, gate_up_full, (((1,), (1,)), ((), ())), preferred_element_type=f32
    )
    back_part = bring_back(back_rows.astype(bf16))
    returned = lax.dot_general(
        act_low, down_full, (((1,), (1,)), ((), ())), preferred_element_type=f32
    )
    output_part = (middle + bring_back(returned.astype(bf16))).astype(bf16)
    rows_in = (((0,), (0,)), ((), ()))
    expert_grads = jnp.concatenate(
        [
            lax.dot_general(rows, pre_grads, rows_in, preferred_element_type=f32),
            lax.dot_general(up_rows, act_low, rows_in, preferred_element_type=f32),
        ],
        axis=1,
    ).astype(bf16)
    expert_grads = lax.all_to_all(
        expert_grads.reshape(EXPERTS, depth, 3 * hidden), both, 0, 0, tiled=True
    ).astype(f32)
    slot_products = lax.psum(slot_products, "tp").reshape(EXPERTS, CAP)
    slot_products = lax.all_to_all(slot_products, both, 0, 0, tiled=True)

    chance_grads = jnp.sum(pick_f32 * slot_products[:, :, None], axis=1).T
    logit_grads = chances * (chance_grads - jnp.sum(chances * chance_grads, axis=-1, keepdims=True))
    scaled_mlp = back_part + jnp.dot(logit_grads, router_part.T, precision=highest)
    inner = lax.psum(jnp.sum(scaled_mlp * middle, axis=-1, keepdims=True), "tp")
    middle_grad = upstream_part + second_rms * scaled_mlp - middle * second_rms**3 / width * inner
    router_term = lax.dot_general(
        normed_mlp.astype(f32), logit_grads, rows_in, precision=highest
    )
    router_term = lax.all_gather(router_term, "tp", axis=0, tiled=True)
    router_term = lax.psum_scatter(router_term, both, scatter_dimension=0, tiled=True)
    grad_router = router_term * mlp_scale[:, None]

    branch_grad = lax.all_gather(middle_grad.astype(bf16), "tp", axis=1, tiled=True)
    grad_out = lax.dot_general(branch_grad, attended, rows_in, preferred_element_type=f32)
    grad_out = lax.psum_scatter(grad_out.astype(bf16), both, scatter_dimension=0, tiled=True)
    attended_grad = jnp.dot(branch_grad, out_all, preferred_element_type=f32).astype(bf16)
    attended_grad = attended_grad.reshape(block, n_ctx, HEAD_DIM).transpose(1, 0, 2)
    attended_grad = lax.all_to_all(attended_grad, "ctx", 0, 0, tiled=True)
    attended_grad = attended_grad.reshape(length, HEAD_DIM)
    prob_grads = jnp.einsum(
        "qd,kd->qk", attended_grad, value_heads, preferred_element_type=f32
    )
    score_grads = (
        probs * (prob_grads - jnp.sum(probs * prob_grads, axis=-1, keepdims=True))
    ).astype(bf16)
    query_grads = jnp.dot(score_grads, key_rot, preferred_element_type=f32) * scale
    key_grads = lax.dot_general(score_grads, query_rot, rows_in, preferred_element_type=f32) * scale
    value_grads = lax.dot_general(probs_low, attended_grad, rows_in, preferred_element_type=f32)
    query_norm_grad = rotate_back(query_grads, cosine, sine_table)
    key_norm_grad = rotate_back(key_grads, cosine, sine_table)
    query_scaled = query_norm_grad * query_gain
    key_scaled = key_norm_grad * key_gain
    inners = lax.psum(
        jnp.stack([jnp.sum(query_scaled * query_proj, axis=-1), jnp.sum(key_scaled * key_proj, axis=-1)]),
        ("ctx", "tp"),
    )
    query_pre = query_rms * query_scaled - query_proj * query_rms**3 / HQ * inners[0][:, None]
    key_pre = key_rms * key_scaled - key_proj * key_rms**3 / HQ * inners[1][:, None]
    gain_terms = jnp.stack(
        [
            jnp.sum(query_norm_grad * query_proj * query_rms, axis=0),
            jnp.sum(key_norm_grad * key_proj * key_rms, axis=0),
        ]
    )
    gain_terms = lax.all_gather(lax.psum(gain_terms, "fsdp"), "ctx", axis=1, tiled=True)
    proj_grads = jnp.concatenate([query_pre, key_pre, value_grads], axis=1).astype(bf16)
    qkv_grads = lax.dot_general(normed, proj_grads, rows_in, preferred_element_type=f32)
    qkv_grads = lax.all_to_all(
        qkv_grads.astype(bf16).reshape(places, depth, 3 * HEAD_DIM), both, 0, 0, tiled=True
    )
    qkv_grads = qkv_grads.astype(f32).reshape(n_fsdp, n_ctx, depth, 3 * HEAD_DIM).sum(axis=0)
    grad_qkv = (qkv_grads * attn_scale[None, :, None]).reshape(n_ctx, depth, 3, HEAD_DIM)
    grad_qkv = grad_qkv.transpose(1, 2, 0, 3).reshape(depth, 3, n_ctx * HEAD_DIM)
    scaled_first = lax.dot_general(
        proj_grads, head_weight, (((1,), (1,)), ((), ())), preferred_element_type=f32
    ).astype(bf16)
    scaled_first = lax.psum_scatter(scaled_first, "tp", scatter_dimension=1, tiled=True)
    scaled_first = lax.psum_scatter(scaled_first, "ctx", scatter_dimension=0, tiled=True)
    scaled_first = scaled_first.astype(f32)
    gains = jnp.stack(
        [
            jnp.sum(qkv_grads * qkv_raw, axis=(0, 2)),
            jnp.sum(expert_grads[:, :, : 2 * hidden] * gate_up_raw.astype(f32), axis=(0, 2)),
        ]
    )
    last_inner = jnp.sum(scaled_first * in_part, axis=-1)
    gains, last_inner = lax.psum((gains, last_inner), "tp")
    grad_mlp_gain = gains[1] + jnp.sum(router_term * router_f32, axis=-1)
    grad_inputs = (
        middle_grad
        + first_rms * scaled_first
        - in_part * first_rms**3 / width * last_inner[:, None]
    )
    grad_inputs = lax.all_gather(grad_inputs.astype(bf16), "tp", axis=1, tiled=True).astype(f32)
    output = lax.all_gather(output_part, "tp", axis=1, tiled=True)
    grad_gate_up = (expert_grads[:, :, : 2 * hidden] * mlp_scale[None, :, None]).reshape(
        EXPERTS, depth, 2, hidden
    )
    return (
        output[None],
        grad_inputs[None],
        gains[0],
        grad_qkv,
        grad_out.astype(f32),
        gain_terms,
        grad_mlp_gain,
        grad_router,
        grad_gate_up.transpose(1, 2, 0, 3),
        expert_grads[:, :, 2 * hidden :].transpose(1, 0, 2),
    )


def solution(mesh):
    sizes = (mesh.shape["fsdp"], mesh.shape["ctx"], mesh.shape["tp"])
    one_expert = sizes[0] * sizes[1] == EXPERTS
    one_head = sizes[1] * sizes[2] * HEAD_DIM == HQ

    def step(*arrays):
        if one_expert and one_head and arrays[0].shape[0] == 1:
            return by_head(sizes, *arrays)
        return on_device(*arrays)

    placed = (
        P("fsdp", "ctx", None),
        P(("fsdp", "ctx")),
        P(("fsdp", "ctx"), None, "tp"),
        P(("fsdp", "ctx"), "tp"),
        P(None, "tp"),
        P(("fsdp", "ctx")),
        P(("fsdp", "ctx"), None),
        P(("fsdp", "ctx"), None, None, "tp"),
        P(("fsdp", "ctx"), None, "tp"),
        P("ctx", "fsdp", None, None),
        P("fsdp", "ctx", None),
    )
    return jax.shard_map(
        step,
        mesh=mesh,
        in_specs=placed,
        out_specs=(
            P("fsdp", "ctx", None),
            P("fsdp", "ctx", None),
            P(("fsdp", "ctx")),
            P(("fsdp", "ctx"), None, "tp"),
            P(("fsdp", "ctx"), "tp"),
            P(None, "tp"),
            P(("fsdp", "ctx")),
            P(("fsdp", "ctx"), None),
            P(("fsdp", "ctx"), None, None, "tp"),
            P(("fsdp", "ctx"), None, "tp"),
        ),
        check_vma=False,
    )
```

```python
import functools
import math

import jax
import jax.numpy as jnp
from jax import lax
from jax.experimental import pallas as pl
from jax.experimental.pallas import tpu as pltpu
from jax.sharding import PartitionSpec as P

HEAD_DIM = 128
TOPK = 4
EXPERTS = 8
HQ = 2048
CAP = 160


epsilon = 1e-05
highest = lax.Precision.HIGHEST


def inv_rms(values):
    return lax.rsqrt(jnp.mean(values * values, axis=-1, keepdims=True) + epsilon)


def rotary_tables(offset, length):
    half_dim = HEAD_DIM // 2
    frequency = jnp.exp(
        jnp.arange(half_dim, dtype=jnp.float32) * (-2.0 * math.log(10000.0) / HEAD_DIM)
    )
    positions = (offset + jnp.arange(length, dtype=jnp.int32)).astype(jnp.float32)
    angles = positions[:, None] * frequency[None, :]
    angles = jnp.concatenate([angles, angles], axis=1)
    return (jnp.cos(angles), jnp.sin(angles))


def rotate(values, cosine, sine_table):
    half_dim = values.shape[-1] // 2
    turned = jnp.concatenate([-values[..., half_dim:], values[..., :half_dim]], axis=-1)
    return values * cosine + turned * sine_table


def rotate_back(grads, cosine, sine_table):
    half_dim = grads.shape[-1] // 2
    scaled = grads * sine_table
    return grads * cosine + jnp.concatenate(
        [scaled[..., half_dim:], -scaled[..., :half_dim]], axis=-1
    )


def slot_table(routed):
    flat_routes = routed.reshape(-1)
    one_hot = (flat_routes[:, None] == jnp.arange(EXPERTS, dtype=jnp.int32)[None, :]).astype(
        jnp.int32
    )
    earlier = jnp.cumsum(one_hot, axis=0) - one_hot
    within = jnp.sum(earlier * one_hot, axis=1)
    slots = flat_routes * CAP + within
    owners = jnp.arange(flat_routes.shape[0], dtype=jnp.int32) // TOPK
    token_of = jnp.zeros((EXPERTS * CAP,), jnp.int32).at[slots].set(owners)
    filled = jnp.zeros((EXPERTS * CAP,), jnp.float32).at[slots].set(1.0)
    return (slots.reshape(routed.shape), token_of, filled)


def on_device(
    inputs,
    attn_gain,
    qkv_weight,
    out_weight,
    qk_gains,
    mlp_gain,
    router_weight,
    gate_up_weight,
    down_weight,
    routes,
    cotangent,
):
    seq_dev, block, width = inputs.shape
    rows = seq_dev * block
    heads_dev = qkv_weight.shape[2] // HEAD_DIM
    scale = 1.0 / math.sqrt(HEAD_DIM)
    place = lax.axis_index("ctx")
    attn_gain_all, qkv_all, out_all, mlp_gain_all, router_all = (
        lax.all_gather(attn_gain, ("fsdp", "ctx"), axis=0, tiled=True),
        lax.all_gather(qkv_weight, ("fsdp", "ctx"), axis=0, tiled=True),
        lax.all_gather(out_weight, ("fsdp", "ctx"), axis=0, tiled=True),
        lax.all_gather(mlp_gain, ("fsdp", "ctx"), axis=0, tiled=True),
        lax.all_gather(router_weight, ("fsdp", "ctx"), axis=0, tiled=True),
    )
    attn_scale = attn_gain_all.astype(jnp.float32)
    mlp_scale = mlp_gain_all.astype(jnp.float32)
    flat_in = inputs.reshape(rows, width).astype(jnp.float32)
    first_rms = inv_rms(flat_in)
    normed = (flat_in * first_rms * attn_scale).astype(jnp.bfloat16)
    projected = jnp.einsum("td,dch->tch", normed, qkv_all, preferred_element_type=jnp.float32)
    query_proj = projected[:, 0]
    key_proj = projected[:, 1]
    query_sums, key_sums = lax.psum(
        (jnp.sum(query_proj * query_proj, axis=-1), jnp.sum(key_proj * key_proj, axis=-1)), "tp"
    )
    query_rms = lax.rsqrt(query_sums / HQ + epsilon)[:, None]
    key_rms = lax.rsqrt(key_sums / HQ + epsilon)[:, None]
    query_gain = qk_gains[0].astype(jnp.float32)
    key_gain = qk_gains[1].astype(jnp.float32)
    query_norm = query_proj * query_rms * query_gain
    key_norm = key_proj * key_rms * key_gain
    cosine, sine_table = rotary_tables(place * block, block)
    cos_heads = cosine[:, None, :]
    sin_heads = sine_table[:, None, :]
    head_shape = (seq_dev, block, heads_dev, HEAD_DIM)
    query_rot = rotate(query_norm.reshape(head_shape), cos_heads, sin_heads).astype(jnp.bfloat16)
    key_rot = rotate(key_norm.reshape(head_shape), cos_heads, sin_heads).astype(jnp.bfloat16)
    value_heads = projected[:, 2].reshape(head_shape).astype(jnp.bfloat16)
    key_all, value_all = (
        lax.all_gather(key_rot, "ctx", axis=1, tiled=True),
        lax.all_gather(value_heads, "ctx", axis=1, tiled=True),
    )
    length = key_all.shape[1]
    key_block = jnp.arange(length, dtype=jnp.int32) // block
    allowed = (key_block <= place)[None, None, None, :]
    scores = (
        jnp.einsum("sqhd,skhd->shqk", query_rot, key_all, preferred_element_type=jnp.float32)
        * scale
    )
    scores = jnp.where(allowed, scores, -1e30)
    top_score = jnp.max(scores, axis=-1, keepdims=True)
    exponent = jnp.exp(scores - top_score)
    total = jnp.sum(exponent, axis=-1, keepdims=True)
    log_total = top_score + jnp.log(total)
    softmaxed = exponent / total
    attended = jnp.einsum(
        "shqk,skhd->sqhd",
        softmaxed.astype(jnp.bfloat16),
        value_all,
        preferred_element_type=jnp.float32,
    )
    attended = attended.reshape(rows, heads_dev * HEAD_DIM).astype(jnp.bfloat16)
    branch = lax.psum(
        jnp.einsum("th,dh->td", attended, out_all, preferred_element_type=jnp.float32), "tp"
    )
    middle = flat_in + branch
    second_rms = inv_rms(middle)
    normed_mlp = (middle * second_rms * mlp_scale).astype(jnp.bfloat16)
    logits = jnp.dot(normed_mlp, router_all, preferred_element_type=jnp.float32)
    chances = jax.nn.softmax(logits, axis=-1)
    routed = routes.reshape(rows, TOPK)
    gates = jnp.take_along_axis(chances, routed, axis=-1)
    slots, token_of, filled = slot_table(routed)
    dispatched = (normed_mlp[token_of] * filled[:, None].astype(jnp.bfloat16)).reshape(
        EXPERTS, CAP, width
    )
    gate_up_all, down_all = (
        lax.all_gather(gate_up_weight, ("fsdp", "ctx"), axis=0, tiled=True),
        lax.all_gather(down_weight, ("fsdp", "ctx"), axis=0, tiled=True),
    )
    gate_up = jnp.einsum(
        "ecd,djef->ecjf", dispatched, gate_up_all, preferred_element_type=jnp.float32
    )
    gate_part = gate_up[:, :, 0]
    up_part = gate_up[:, :, 1]
    activated = (jax.nn.silu(gate_part) * up_part).astype(jnp.bfloat16)
    upstream = cotangent.reshape(rows, width).astype(jnp.float32)
    slot_gates = (
        jnp.zeros((EXPERTS * CAP,), jnp.float32)
        .at[slots.reshape(-1)]
        .set(gates.reshape(-1))
        .reshape(EXPERTS, CAP)
    )
    token_grid = token_of.reshape(EXPERTS, CAP)
    filled_grid = filled.reshape(EXPERTS, CAP)

    def expert_forward(expert_index, running):
        combined, slot_products = running
        expert_down = lax.dynamic_index_in_dim(down_all, expert_index, 1, keepdims=False)
        expert_act = lax.dynamic_index_in_dim(activated, expert_index, 0, keepdims=False)
        expert_tokens = lax.dynamic_index_in_dim(token_grid, expert_index, 0, keepdims=False)
        expert_gates = lax.dynamic_index_in_dim(slot_gates, expert_index, 0, keepdims=False)
        returned_rows = jnp.einsum(
            "cf,df->cd", expert_act, expert_down, preferred_element_type=jnp.float32
        )
        combined = combined.at[expert_tokens].add(returned_rows * expert_gates[:, None])
        products = jnp.sum(returned_rows * upstream[expert_tokens], axis=-1)
        slot_products = lax.dynamic_update_index_in_dim(slot_products, products, expert_index, 0)
        return (combined, slot_products)

    combined, slot_products = lax.fori_loop(
        0,
        EXPERTS,
        expert_forward,
        (jnp.zeros((rows, width), jnp.float32), jnp.zeros((EXPERTS, CAP), jnp.float32)),
    )
    gate_grad_part = slot_products.reshape(-1)[slots]
    expert_sum = lax.psum(combined, "tp")
    output = (middle + expert_sum).astype(jnp.bfloat16).reshape(seq_dev, block, width)
    slot_grads = (
        (slot_gates.reshape(-1)[:, None] * upstream[token_of])
        .astype(jnp.bfloat16)
        .reshape(EXPERTS, CAP, width)
    )
    gate_up_back, down_back = (
        lax.all_gather(gate_up_weight, ("fsdp", "ctx"), axis=0, tiled=True),
        lax.all_gather(down_weight, ("fsdp", "ctx"), axis=0, tiled=True),
    )
    act_grads = jnp.einsum(
        "ecd,def->ecf", slot_grads, down_back, preferred_element_type=jnp.float32
    )
    sigmoid = jax.nn.sigmoid(gate_part)
    gate_grads = act_grads * up_part * sigmoid * (1.0 + gate_part * (1.0 - sigmoid))
    up_grads = act_grads * (gate_part * sigmoid)
    pre_grads = jnp.stack([gate_grads, up_grads], axis=2).astype(jnp.bfloat16)

    def expert_backward(expert_index, running):
        expert_pre = lax.dynamic_index_in_dim(pre_grads, expert_index, 0, keepdims=False)
        expert_weight = lax.dynamic_index_in_dim(gate_up_back, expert_index, 2, keepdims=False)
        expert_tokens = lax.dynamic_index_in_dim(token_grid, expert_index, 0, keepdims=False)
        expert_filled = lax.dynamic_index_in_dim(filled_grid, expert_index, 0, keepdims=False)
        expert_back = jnp.einsum(
            "cjf,djf->cd", expert_pre, expert_weight, preferred_element_type=jnp.float32
        )
        return running.at[expert_tokens].add(expert_back * expert_filled[:, None])

    expert_input_part = lax.fori_loop(
        0, EXPERTS, expert_backward, jnp.zeros((rows, width), jnp.float32)
    )
    gate_up_term = jnp.einsum(
        "ecd,ecjf->djef", dispatched, pre_grads, preferred_element_type=jnp.float32
    )
    down_term = jnp.einsum(
        "ecf,ecd->def", activated, slot_grads, preferred_element_type=jnp.float32
    )
    expert_grads = lax.psum_scatter(
        jnp.concatenate([gate_up_term, down_term[:, None]], axis=1),
        ("fsdp", "ctx"),
        scatter_dimension=0,
        tiled=True,
    )
    gate_up_share = expert_grads[:, :2]
    down_share = expert_grads[:, 2]
    expert_input, gate_total = lax.psum((expert_input_part, gate_grad_part), "tp")
    chosen = (routed[:, :, None] == jnp.arange(EXPERTS, dtype=jnp.int32)[None, None, :]).astype(
        jnp.float32
    )
    chance_grads = jnp.sum(gate_total[:, :, None] * chosen, axis=1)
    logit_grads = chances * (chance_grads - jnp.sum(chances * chance_grads, axis=-1, keepdims=True))
    router_f32 = router_all.astype(jnp.float32)
    mlp_input = expert_input + jnp.dot(logit_grads, router_f32.T, precision=highest)
    grad_router = jnp.dot(normed_mlp.astype(jnp.float32).T, logit_grads, precision=highest)
    grad_mlp_gain = jnp.sum(mlp_input * middle * second_rms, axis=0)
    scaled_mlp = mlp_input * mlp_scale
    middle_grad = (
        upstream
        + second_rms * scaled_mlp
        - middle * second_rms**3 / width * jnp.sum(scaled_mlp * middle, axis=-1, keepdims=True)
    )
    branch_grad = middle_grad.astype(jnp.bfloat16)
    grad_out = jnp.einsum("td,th->dh", branch_grad, attended, preferred_element_type=jnp.float32)
    attended_grad = (
        jnp.dot(branch_grad, out_all, preferred_element_type=jnp.float32)
        .astype(jnp.bfloat16)
        .reshape(head_shape)
    )
    again_scores = (
        jnp.einsum("sqhd,skhd->shqk", query_rot, key_all, preferred_element_type=jnp.float32)
        * scale
    )
    again_scores = jnp.where(allowed, again_scores, -1e30)
    recomputed = jnp.exp(again_scores - log_total)
    prob_grads = jnp.einsum(
        "sqhd,skhd->shqk", attended_grad, value_all, preferred_element_type=jnp.float32
    )
    score_grads = (
        recomputed * (prob_grads - jnp.sum(recomputed * prob_grads, axis=-1, keepdims=True))
    ).astype(jnp.bfloat16)
    query_grads = (
        jnp.einsum("shqk,skhd->sqhd", score_grads, key_all, preferred_element_type=jnp.float32)
        * scale
    )
    key_grads = (
        jnp.einsum("shqk,sqhd->skhd", score_grads, query_rot, preferred_element_type=jnp.float32)
        * scale
    )
    value_grads = jnp.einsum(
        "shqk,sqhd->skhd",
        recomputed.astype(jnp.bfloat16),
        attended_grad,
        preferred_element_type=jnp.float32,
    )
    key_back, value_back = (
        lax.psum_scatter(key_grads, "ctx", scatter_dimension=1, tiled=True),
        lax.psum_scatter(value_grads, "ctx", scatter_dimension=1, tiled=True),
    )
    query_norm_grad = rotate_back(query_grads, cos_heads, sin_heads).reshape(rows, -1)
    key_norm_grad = rotate_back(key_back, cos_heads, sin_heads).reshape(rows, -1)
    query_scaled = query_norm_grad * query_gain
    key_scaled = key_norm_grad * key_gain
    query_inner, key_inner = lax.psum(
        (jnp.sum(query_scaled * query_proj, axis=-1), jnp.sum(key_scaled * key_proj, axis=-1)), "tp"
    )
    query_pre = query_rms * query_scaled - query_proj * query_rms**3 / HQ * query_inner[:, None]
    key_pre = key_rms * key_scaled - key_proj * key_rms**3 / HQ * key_inner[:, None]
    gain_terms = jnp.stack(
        [
            jnp.sum(query_norm_grad * query_proj * query_rms, axis=0),
            jnp.sum(key_norm_grad * key_proj * key_rms, axis=0),
        ]
    )
    grad_qk_gains = lax.psum(gain_terms, ("fsdp", "ctx"))
    proj_grads = jnp.stack([query_pre, key_pre, value_back.reshape(rows, -1)], axis=1).astype(
        jnp.bfloat16
    )
    grad_qkv = jnp.einsum("td,tch->dch", normed, proj_grads, preferred_element_type=jnp.float32)
    normed_grad = lax.psum(
        jnp.einsum("tch,dch->td", proj_grads, qkv_all, preferred_element_type=jnp.float32), "tp"
    )
    grad_attn_gain = jnp.sum(normed_grad * flat_in * first_rms, axis=0)
    scaled_first = normed_grad * attn_scale
    grad_inputs = (
        middle_grad
        + first_rms * scaled_first
        - flat_in * first_rms**3 / width * jnp.sum(scaled_first * flat_in, axis=-1, keepdims=True)
    )
    shares = (
        lax.psum_scatter(grad_attn_gain, ("fsdp", "ctx"), scatter_dimension=0, tiled=True),
        lax.psum_scatter(grad_qkv, ("fsdp", "ctx"), scatter_dimension=0, tiled=True),
        lax.psum_scatter(grad_out, ("fsdp", "ctx"), scatter_dimension=0, tiled=True),
        lax.psum_scatter(grad_mlp_gain, ("fsdp", "ctx"), scatter_dimension=0, tiled=True),
        lax.psum_scatter(grad_router, ("fsdp", "ctx"), scatter_dimension=0, tiled=True),
    )
    return (
        output,
        grad_inputs.reshape(seq_dev, block, width),
        shares[0],
        shares[1],
        shares[2],
        grad_qk_gains,
        shares[3],
        shares[4],
        gate_up_share,
        down_share,
    )


MESH = pl.DeviceIdType.MESH


def remote(src, dst, send, recv, **where):
    return pltpu.make_async_remote_copy(
        src_ref=src, dst_ref=dst, send_sem=send, recv_sem=recv, device_id=where, device_id_type=MESH
    )


def greet(peers):
    barrier = pltpu.get_barrier_semaphore()
    for where in peers:
        pl.semaphore_signal(barrier, inc=1, device_id=where, device_id_type=MESH)
    pl.semaphore_wait(barrier, len(peers))


def in_group(sizes, step):
    _, n_ctx, n_tp = sizes
    here = lax.axis_index("ctx") * n_tp + lax.axis_index("tp")
    there = lax.rem(here + step, n_ctx * n_tp)
    return {"ctx": there // n_tp, "tp": lax.rem(there, n_tp)}, there


def rows_at(place, size):
    return pl.ds(pl.multiple_of(place * size, size), size)


def dot_f32(a, b, dims, precision=None):
    return lax.dot_general(
        a, b, (dims, ((), ())), precision=precision, preferred_element_type=jnp.float32
    )


def group_sum(sizes, own, parts, send, recv):
    _, n_ctx, n_tp = sizes
    others = n_ctx * n_tp - 1
    here = lax.axis_index("ctx") * n_tp + lax.axis_index("tp")
    copies = []
    for step in range(1, others + 1):
        where, _ = in_group(sizes, step)
        copies.append(remote(own, parts.at[here], send.at[step - 1], recv.at[step - 1], **where))
        copies[-1].start()
    total = own[...]
    for step in range(1, others + 1):
        copies[step - 1].wait_recv()
        _, there = in_group(sizes, others + 1 - step)
        total = total + parts[there]
    for copy in copies:
        copy.wait_send()
    return total


def attend_kernel(
    sizes,
    scale,
    own_rows,
    weight,
    gains,
    cosine,
    sine,
    own_router,
    normed,
    head_weight,
    query_proj,
    key_proj,
    query_rot,
    key_rot,
    value,
    rms,
    attended,
    router,
    own_attended,
    own_sums,
    sums,
    w_send,
    w_recv,
    x_send,
    x_recv,
    n_send,
    n_recv,
    y_send,
    y_recv,
    c_send,
    c_recv,
    s_send,
    s_recv,
    a_send,
    a_recv,
    r_send,
    r_recv,
):
    n_fsdp, n_ctx, n_tp = sizes
    fsdp, ctx, tp = lax.axis_index("fsdp"), lax.axis_index("ctx"), lax.axis_index("tp")
    block = own_rows.shape[0]
    share = block // n_tp
    half_dim = HEAD_DIM // 2
    mate = tp + 1 - 2 * lax.rem(tp, 2)
    over = lax.rem(tp + 2, n_tp)
    over_mate = lax.rem(mate + 2, n_tp)
    across = 1 - fsdp
    places = n_fsdp * n_ctx
    me = fsdp * n_ctx + ctx
    greet(
        [in_group(sizes, step)[0] for step in range(1, n_ctx * n_tp)]
        + [
            {"fsdp": across, "ctx": lax.rem(ctx + step, n_ctx)}
            for step in range(n_ctx)
        ]
    )

    copies = []

    def go(*args, **where):
        copy = remote(*args, **where)
        copy.start()
        copies.append(copy)
        return copy

    def back(step):
        return lax.rem(ctx + n_ctx - step, n_ctx)

    mine = rows_at(tp, share)
    from_w, from_n, from_y, from_c, from_x = {}, {}, {}, {}, {}
    for step in range(1, n_ctx):
        there = lax.rem(ctx + step, n_ctx)
        from_w[step] = go(
            weight.at[there],
            head_weight.at[fsdp * n_ctx + ctx],
            w_send.at[step - 1],
            w_recv.at[step - 1],
            ctx=there,
        )
    from_x[0] = go(
        weight.at[ctx],
        head_weight.at[fsdp * n_ctx + ctx],
        x_send.at[0],
        x_recv.at[0],
        fsdp=across,
    )
    for step in range(1, n_ctx):
        there = lax.rem(ctx + step, n_ctx)
        from_n[step] = go(
            own_rows.at[mine], normed.at[ctx, mine], n_send.at[step - 1], n_recv.at[step - 1], ctx=there
        )
    from_r = []
    for step in range(1, places):
        there = later(sizes, step)
        from_r.append(
            go(
                own_router,
                router.at[me],
                r_send.at[step - 1],
                r_recv.at[step - 1],
                **place_at(sizes, there),
            )
        )
    router[me] = own_router[...]
    head_weight[fsdp * n_ctx + ctx] = weight[ctx]
    normed[ctx] = own_rows[...]
    for step in range(1, n_ctx):
        origin = back(step)
        from_w[step].wait_recv()
        piece = head_weight.at[fsdp * n_ctx + origin]
        from_x[step] = go(piece, piece, x_send.at[step], x_recv.at[step], fsdp=across)
        from_n[step].wait_recv()
        piece = normed.at[origin, mine]
        from_y[step] = go(piece, piece, y_send.at[step - 1], y_recv.at[step - 1], tp=over)
        from_c[step, 0] = go(
            piece, piece, c_send.at[step - 1, 0], c_recv.at[step - 1, 0], tp=mate
        )
    for step in range(1, n_ctx):
        from_y[step].wait_recv()
        piece = normed.at[back(step), rows_at(over, share)]
        from_c[step, 1] = go(
            piece, piece, c_send.at[step - 1, 1], c_recv.at[step - 1, 1], tp=mate
        )
    for step in range(n_ctx):
        from_x[step].wait_recv()

    width = head_weight.shape[0] * head_weight.shape[1]
    line = lax.broadcasted_iota(jnp.int32, own_sums.shape, 0)
    ones = jnp.ones((2 * n_ctx, HEAD_DIM), jnp.float32)
    all_sums = jnp.zeros(own_sums.shape, jnp.float32)
    for step in range(n_ctx):
        if step:
            from_c[step, 0].wait_recv()
            from_c[step, 1].wait_recv()
        origin = back(step)
        here = rows_at(origin, block)
        projected = dot_f32(
            normed[origin], head_weight[...].reshape(width, 3 * HEAD_DIM), ((1,), (0,))
        )
        query, key = projected[:, :HEAD_DIM], projected[:, HEAD_DIM : 2 * HEAD_DIM]
        query_proj[here] = query
        key_proj[here] = key
        value[here] = projected[:, 2 * HEAD_DIM :].astype(value.dtype)
        query_sum = dot_f32(ones, query * query, ((1,), (1,)), highest)
        key_sum = dot_f32(ones, key * key, ((1,), (1,)), highest)
        all_sums = jnp.where(line == origin, query_sum, all_sums)
        all_sums = jnp.where(line == origin + n_ctx, key_sum, all_sums)
    own_sums[...] = all_sums
    total = group_sum(sizes, own_sums, sums, s_send, s_recv)
    inverse = lax.rsqrt(total / HQ + epsilon)
    columns = inverse.T
    rms[...] = columns
    for place in range(n_ctx):
        here = slice(place * block, (place + 1) * block)
        cos_here, sin_here = cosine[here], sine[here]
        for proj, rot, which in ((query_proj, query_rot, 0), (key_proj, key_rot, 1)):
            scaled = proj[here] * columns[:, which * n_ctx + place][:, None] * gains[which]
            turned = pltpu.roll(scaled, half_dim, 1)
            rot[here] = (scaled * cos_here + turned * sin_here).astype(rot.dtype)
    from_a = {}
    for place in range(n_ctx):
        here = slice(place * block, (place + 1) * block)
        seen = slice(0, (place + 1) * block)
        scores = dot_f32(query_rot[here], key_rot[seen], ((1,), (1,))) * scale
        exponent = jnp.exp(scores - jnp.max(scores, axis=-1, keepdims=True))
        probs = exponent / jnp.sum(exponent, axis=-1, keepdims=True)
        mixed = dot_f32(probs.astype(value.dtype), value[seen], ((1,), (0,)))
        own_attended[place] = mixed.astype(own_attended.dtype)
        lanes = rows_at(ctx, HEAD_DIM)
        from_a[place] = remote(
            own_attended.at[place],
            attended.at[:, lanes],
            a_send.at[place],
            a_recv.at[ctx],
            ctx=place,
        )

        @pl.when(ctx != place)
        def _():
            from_a[place].start()

        @pl.when(ctx == place)
        def _():
            attended[:, lanes] = own_attended[place]

    for place in range(n_ctx):

        @pl.when(ctx != place)
        def _():
            from_a[place].wait_send()
            remote(
                own_attended.at[place],
                attended.at[:, rows_at(place, HEAD_DIM)],
                a_send.at[place],
                a_recv.at[place],
                ctx=place,
            ).wait_recv()

    for copy in from_r:
        copy.wait_recv()
    for copy in copies:
        copy.wait_send()


def attend(sizes, own_rows, weight, gains, cosine, sine, router):
    n_fsdp, n_ctx, n_tp = sizes
    block, width = own_rows.shape
    _, depth, columns = weight.shape
    length = n_ctx * block
    group = n_ctx * n_tp
    bf16, f32 = jnp.bfloat16, jnp.float32
    vmem = pl.BlockSpec(memory_space=pltpu.VMEM)
    dma = pltpu.SemaphoreType.DMA
    shape = jax.ShapeDtypeStruct
    outs = (
        shape((n_ctx, block, width), bf16),
        shape((n_fsdp * n_ctx, depth, columns), bf16),
        shape((length, HEAD_DIM), f32),
        shape((length, HEAD_DIM), f32),
        shape((length, HEAD_DIM), bf16),
        shape((length, HEAD_DIM), bf16),
        shape((length, HEAD_DIM), bf16),
        shape((block, 2 * n_ctx), f32),
        shape((block, n_ctx * HEAD_DIM), bf16),
        shape((n_fsdp * n_ctx,) + router.shape, f32),
    )
    pairs = [
        (n_ctx - 1,),
        (n_ctx,),
        (n_ctx - 1,),
        (n_ctx - 1,),
        (n_ctx - 1, 2),
        (group - 1,),
        (n_ctx,),
        (n_fsdp * n_ctx - 1,),
    ]
    return pl.pallas_call(
        functools.partial(attend_kernel, sizes, 1.0 / math.sqrt(HEAD_DIM)),
        name="attend",
        out_shape=outs,
        in_specs=[vmem] * 6,
        out_specs=(vmem,) * len(outs),
        scratch_shapes=[
            pltpu.VMEM((n_ctx, block, HEAD_DIM), bf16),
            pltpu.VMEM((2 * n_ctx, block), f32),
            pltpu.VMEM((group, 2 * n_ctx, block), f32),
        ]
        + [dma(size) for size in pairs for _ in range(2)],
        compiler_params=pltpu.CompilerParams(collective_id=0, has_side_effects=True),
        cost_estimate=pl.CostEstimate(
            flops=70_000_000_000, bytes_accessed=20_000_000, transcendentals=1_000_000
        ),
    )(own_rows, weight, gains, cosine, sine, router)


def signed_tables(offset, length):
    cosine, sine = rotary_tables(offset, length)
    half_dim = HEAD_DIM // 2
    return cosine, jnp.concatenate([-sine[:, :half_dim], sine[:, half_dim:]], axis=1)


def around(sizes):
    n_fsdp, n_ctx, n_tp = sizes
    me = lax.axis_index("fsdp") * n_ctx + lax.axis_index("ctx")
    tp = lax.axis_index("tp")
    mate = tp + 1 - 2 * lax.rem(tp, 2)
    over = lax.rem(tp + 2, n_tp)
    return me, tp, mate, over, lax.rem(mate + 2, n_tp)


def place_at(sizes, place):
    return {"fsdp": place // sizes[1], "ctx": lax.rem(place, sizes[1])}


def later(sizes, step):
    places = sizes[0] * sizes[1]
    me = lax.axis_index("fsdp") * sizes[1] + lax.axis_index("ctx")
    return lax.rem(me + step, places)


def tp_sum(own, parts, send, recv, peers):
    copies = [
        remote(own, parts.at[i], send.at[i], recv.at[i], tp=peer) for i, peer in enumerate(peers)
    ]
    for copy in copies:
        copy.start()
    total = own[...]
    for i, copy in enumerate(copies):
        copy.wait_recv()
        total = total + parts[i]
    for copy in copies:
        copy.wait_send()
    return total


def middle_kernel(
    sizes,
    attended,
    out_all,
    in_part,
    router,
    pick,
    middle,
    small,
    chances,
    normed,
    rows,
    gates,
    c_out,
    c_in,
    y_out,
    y_in,
    own_small,
    smalls,
    rows_out,
    gates_out,
    m_send,
    m_recv,
    t_send,
    t_recv,
    z_send,
    z_recv,
    g_send,
    g_recv,
    y_send,
    y_recv,
    c_send,
    c_recv,
    d_send,
    d_recv,
):
    bf16, f32 = jnp.bfloat16, jnp.float32
    n_fsdp, n_ctx, n_tp = sizes
    places = n_fsdp * n_ctx
    me, tp, mate, over, over_mate = around(sizes)
    quarter = in_part.shape[1]
    width = quarter * n_tp
    per = places // n_tp
    greet(
        [{"tp": peer} for peer in (mate, over, over_mate)]
        + [place_at(sizes, later(sizes, step)) for step in range(1, places)]
    )

    def branch(which):
        return dot_f32(attended[...], out_all[rows_at(which, quarter)], ((1,), (1,)))

    to_mate = []
    for i, which in enumerate((over_mate, mate)):
        c_out[i] = branch(which).astype(bf16)
        to_mate.append(remote(c_out.at[i], c_in.at[i], m_send.at[i], m_recv.at[i], tp=mate))
        to_mate[i].start()
    part = branch(over)
    to_mate[0].wait_recv()
    y_out[...] = (part + c_in[0].astype(f32)).astype(bf16)
    to_over = remote(y_out, y_in, m_send.at[2], m_recv.at[2], tp=over)
    to_over.start()
    part = in_part[...] + branch(tp)
    to_mate[1].wait_recv()
    part = part + c_in[1].astype(f32)
    to_over.wait_recv()
    part = part + y_in[...].astype(f32)
    for copy in (*to_mate, to_over):
        copy.wait_send()
    middle[...] = part

    depth = quarter // per
    raw = jnp.zeros((EXPERTS, part.shape[0]), f32)
    for i in range(per):
        raw = raw + dot_f32(
            router[tp * per + i], part[:, i * depth : (i + 1) * depth], ((1,), (1,)), highest
        )
    own_small[:EXPERTS] = raw
    own_small[EXPERTS:] = dot_f32(jnp.ones((8, quarter), f32), part * part, ((1,), (1,)), highest)
    total = tp_sum(own_small, smalls, t_send, t_recv, (mate, over, over_mate))
    inverse = lax.rsqrt(total[EXPERTS:] / width + epsilon)
    small[:EXPERTS] = total[:EXPERTS]
    small[EXPERTS:] = inverse
    logits = total[:EXPERTS] * inverse[:1]
    exponent = jnp.exp(logits - jnp.max(logits, axis=0, keepdims=True))
    chances[...] = exponent / jnp.sum(exponent, axis=0, keepdims=True)
    normed[...] = (part * inverse.T[:, :1]).astype(bf16)

    lanes = rows_at(tp, quarter)
    over_lanes = rows_at(over, quarter)

    def own_row(step):
        return remote(
            rows_out.at[later(sizes, step)],
            rows.at[me, :, lanes],
            z_send.at[step],
            z_recv.at[step],
            **place_at(sizes, later(sizes, step)),
        )

    def own_gate(step):
        return remote(
            gates_out.at[later(sizes, step)],
            gates.at[me],
            g_send.at[step],
            g_recv.at[step],
            **place_at(sizes, later(sizes, step)),
        )

    def onward(step, which, send, recv, peer):
        piece = rows.at[later(sizes, places - step), :, which]
        return remote(piece, piece, send.at[step], recv.at[step], tp=peer)

    def to_y(step):
        return onward(step, lanes, y_send, y_recv, over)

    def to_c(step):
        return onward(step, lanes, c_send, c_recv, mate)

    def to_d(step):
        return onward(step, over_lanes, d_send, d_recv, mate)

    def build(step, carry):
        there = later(sizes, step)
        rows_out[there] = dot_f32(pick[there], normed[...], ((1,), (0,))).astype(bf16)
        chance = jnp.broadcast_to(chances[pl.ds(there, 1)], (8, chances.shape[1]))
        gates_out[there, :, :CAP] = dot_f32(
            chance, pick[there].astype(f32), ((1,), (1,)), highest
        )

        @pl.when(step < places)
        def _():
            own_row(step).start()
            own_gate(step).start()

        return carry

    gates_out[...] = jnp.zeros_like(gates_out)
    lax.fori_loop(1, places + 1, build, 0)
    rows[me, :, lanes] = rows_out[me]
    gates[me] = gates_out[me]
    to_y(0).start()
    to_c(0).start()

    def pass_on(step, carry):
        own_row(step).wait_recv()
        to_y(step).start()
        to_c(step).start()
        to_y(step - 1).wait_recv()
        to_d(step - 1).start()
        return carry

    lax.fori_loop(1, places, pass_on, 0)
    to_y(places - 1).wait_recv()
    to_d(places - 1).start()

    def finish(step, carry):
        to_c(step).wait_recv()
        to_d(step).wait_recv()
        to_c(step).wait_send()
        to_d(step).wait_send()
        to_y(step).wait_send()

        @pl.when(step > 0)
        def _():
            own_row(step).wait_send()
            own_gate(step).wait()

        return carry

    lax.fori_loop(0, places, finish, 0)


def middle_stage(sizes, attended, out_all, in_part, router, pick):
    n_fsdp, n_ctx, n_tp = sizes
    places = n_fsdp * n_ctx
    block, quarter = in_part.shape
    bf16, f32 = jnp.bfloat16, jnp.float32
    vmem = pl.BlockSpec(memory_space=pltpu.VMEM)
    dma = pltpu.SemaphoreType.DMA
    shape = jax.ShapeDtypeStruct
    outs = (
        shape((block, quarter), f32),
        shape((EXPERTS + 8, block), f32),
        shape((EXPERTS, block), f32),
        shape((block, quarter), bf16),
        shape((places, CAP, quarter * n_tp), bf16),
        shape((places, 8, block), f32),
    )
    pairs = [3, 3, places, places, places, places, places]
    return pl.pallas_call(
        functools.partial(middle_kernel, sizes),
        name="middle",
        out_shape=outs,
        in_specs=[vmem] * 5,
        out_specs=(vmem,) * len(outs),
        scratch_shapes=[
            pltpu.VMEM((2, block, quarter), bf16),
            pltpu.VMEM((2, block, quarter), bf16),
            pltpu.VMEM((block, quarter), bf16),
            pltpu.VMEM((block, quarter), bf16),
            pltpu.VMEM((EXPERTS + 8, block), f32),
            pltpu.VMEM((3, EXPERTS + 8, block), f32),
            pltpu.VMEM((places, CAP, quarter), bf16),
            pltpu.VMEM((places, 8, block), f32),
        ]
        + [dma((size,)) for size in pairs for _ in range(2)],
        compiler_params=pltpu.CompilerParams(collective_id=1, has_side_effects=True),
        cost_estimate=pl.CostEstimate(
            flops=60_000_000_000, bytes_accessed=20_000_000, transcendentals=1_000_000
        ),
    )(attended, out_all, in_part, router, pick)


def expert_kernel(
    sizes,
    rows,
    up_rows,
    weight,
    gates,
    back,
    products,
    act_low,
    pre_grads,
    returned,
    keep,
    c_out,
    c_in,
    y_out,
    y_in,
    z_out,
    p_out,
    c_send,
    c_recv,
    y_send,
    y_recv,
    z_send,
    z_recv,
    p_send,
    p_recv,
):
    bf16, f32 = jnp.bfloat16, jnp.float32
    n_fsdp, n_ctx, n_tp = sizes
    places = n_fsdp * n_ctx
    me, tp, mate, over, over_mate = around(sizes)
    width = rows.shape[2]
    quarter = width // n_tp
    hidden = weight.shape[1] // 3
    greet(
        [{"tp": mate}, {"tp": over}]
        + [place_at(sizes, later(sizes, step)) for step in range(1, places)]
    )

    def to_mate(i):
        return remote(c_out.at[i], c_in.at[i], c_send.at[i], c_recv.at[i], tp=mate)

    def to_over(i):
        return remote(y_out.at[i], y_in.at[i], y_send.at[i], y_recv.at[i], tp=over)

    def home(i):
        there = later(sizes, i + 1)
        return remote(
            z_out.at[i], back.at[me], z_send.at[i], z_recv.at[i], **place_at(sizes, there)
        )

    def home_products(i):
        there = later(sizes, i + 1)
        return remote(
            p_out.at[i], products.at[me], p_send.at[i], p_recv.at[i], **place_at(sizes, there)
        )

    def second(i):
        to_mate(i).wait_recv()
        y_out[i] = (keep[i, 0] + c_in[i, 0].astype(f32)).astype(bf16)
        to_over(i).start()

    def third(i):
        to_over(i).wait_recv()
        z_out[i] = (keep[i, 1] + c_in[i, 1].astype(f32) + y_in[i].astype(f32)).astype(bf16)

        @pl.when(i < places - 1)
        def _():
            home(i).start()

        @pl.when(i == places - 1)
        def _():
            back[me] = z_out[i]

    p_out[...] = jnp.zeros_like(p_out)

    def first(i, carry):
        there = later(sizes, i + 1)
        gate_up = dot_f32(rows[there], weight[:, : 2 * hidden], ((1,), (0,)))
        act_grads = dot_f32(up_rows[there], weight[:, 2 * hidden :], ((1,), (0,)))
        gate_part, up_part = gate_up[:, :hidden], gate_up[:, hidden:]
        slot_gates = gates[there].T[:CAP, :1]
        sigmoid = 1.0 / (1.0 + jnp.exp(-gate_part))
        silu = gate_part * sigmoid
        activated = silu * up_part
        act = (activated * slot_gates).astype(bf16)
        p_out[i, :, :CAP] = dot_f32(
            jnp.ones((8, hidden), f32), activated * act_grads, ((1,), (1,)), highest
        )
        gated = act_grads * slot_gates
        pre = jnp.concatenate(
            [gated * up_part * sigmoid * (1.0 + gate_part * (1.0 - sigmoid)), gated * silu], axis=1
        ).astype(bf16)
        act_low[there] = act
        pre_grads[there] = pre

        def input_part(which):
            return dot_f32(pre, weight[rows_at(which, quarter), : 2 * hidden], ((1,), (1,)))

        c_out[i, 0] = input_part(over_mate).astype(bf16)
        c_out[i, 1] = input_part(mate).astype(bf16)
        to_mate(i).start()
        keep[i, 0] = input_part(over)
        keep[i, 1] = input_part(tp)

        @pl.when(i < places - 1)
        def _():
            home_products(i).start()

        @pl.when(i == places - 1)
        def _():
            products[me] = p_out[i]

        @pl.when(i > 0)
        def _():
            second(i - 1)

        returned[there] = dot_f32(act, weight[:, 2 * hidden :], ((1,), (1,))).astype(bf16)

        @pl.when(i > 1)
        def _():
            third(i - 2)

        return carry

    lax.fori_loop(0, places, first, 0)
    second(places - 1)
    third(places - 2)
    third(places - 1)

    def finish(i, carry):
        to_mate(i).wait_send()
        to_over(i).wait_send()

        @pl.when(i < places - 1)
        def _():
            home(i).wait()
            home_products(i).wait()

        return carry

    lax.fori_loop(0, places, finish, 0)


def expert_stage(sizes, rows, up_rows, weight, gates):
    n_fsdp, n_ctx, n_tp = sizes
    places, _, width = rows.shape
    quarter = width // n_tp
    hidden = weight.shape[1] // 3
    bf16, f32 = jnp.bfloat16, jnp.float32
    vmem = pl.BlockSpec(memory_space=pltpu.VMEM)
    dma = pltpu.SemaphoreType.DMA
    shape = jax.ShapeDtypeStruct
    outs = (
        shape((places, CAP, quarter), bf16),
        shape(gates.shape, f32),
        shape((places, CAP, hidden), bf16),
        shape((places, CAP, 2 * hidden), bf16),
        shape((places, CAP, width), bf16),
    )
    return pl.pallas_call(
        functools.partial(expert_kernel, sizes),
        name="expert",
        out_shape=outs,
        in_specs=[vmem] * 4,
        out_specs=(vmem,) * len(outs),
        scratch_shapes=[
            pltpu.VMEM((places, 2, CAP, quarter), f32),
            pltpu.VMEM((places, 2, CAP, quarter), bf16),
            pltpu.VMEM((places, 2, CAP, quarter), bf16),
            pltpu.VMEM((places, CAP, quarter), bf16),
            pltpu.VMEM((places, CAP, quarter), bf16),
            pltpu.VMEM((places, CAP, quarter), bf16),
            pltpu.VMEM(gates.shape, f32),
        ]
        + [dma((places,)) for _ in range(8)],
        compiler_params=pltpu.CompilerParams(collective_id=2, has_side_effects=True),
        cost_estimate=pl.CostEstimate(
            flops=50_000_000_000, bytes_accessed=30_000_000, transcendentals=1_000_000
        ),
    )(rows, up_rows, weight, gates)


def attend_scores(query_rot, key_rot, scale, block):
    scores = jnp.einsum("qd,kd->qk", query_rot, key_rot, preferred_element_type=jnp.float32) * scale
    length = scores.shape[0]
    place = jnp.arange(length, dtype=jnp.int32) // block
    return jnp.where(place[None, :] <= place[:, None], scores, -1e30)


def by_head(
    sizes,
    inputs,
    attn_gain,
    qkv_weight,
    out_weight,
    qk_gains,
    mlp_gain,
    router_weight,
    gate_up_weight,
    down_weight,
    routes,
    cotangent,
):
    n_fsdp, n_ctx, n_tp = sizes
    places = n_fsdp * n_ctx
    both = ("fsdp", "ctx")
    f32, bf16 = jnp.float32, jnp.bfloat16
    _, block, width = inputs.shape
    depth = width // places
    quarter = width // n_tp
    length = n_ctx * block
    hidden = gate_up_weight.shape[3]
    scale = 1.0 / math.sqrt(HEAD_DIM)
    ctx, tp = lax.axis_index("ctx"), lax.axis_index("tp")

    def own_quarter(values):
        return lax.dynamic_slice_in_dim(values, tp * quarter, quarter, axis=1)

    attn_scale = attn_gain.astype(f32)
    mlp_scale = mlp_gain.astype(f32)
    qkv_raw = qkv_weight.reshape(depth, 3, n_ctx, HEAD_DIM).transpose(2, 0, 1, 3)
    qkv_raw = qkv_raw.reshape(n_ctx, depth, 3 * HEAD_DIM).astype(f32)
    qkv_scaled = (qkv_raw * attn_scale[None, :, None]).astype(bf16)
    gate_up_raw = gate_up_weight.transpose(2, 0, 1, 3).reshape(EXPERTS, depth, 2 * hidden)
    down_raw = down_weight.transpose(1, 0, 2)
    expert_send = jnp.concatenate(
        [(gate_up_raw.astype(f32) * mlp_scale[None, :, None]).astype(bf16), down_raw], axis=2
    )
    expert_weight = lax.all_to_all(expert_send, both, 0, 0, tiled=True)
    expert_weight = expert_weight.reshape(width, 3 * hidden)
    out_all = lax.all_gather(out_weight, both, axis=0, tiled=True)
    router_f32 = router_weight.astype(f32)
    router_own = (router_f32 * mlp_scale[:, None]).T

    routed = routes.reshape(block, TOPK)
    named = (routed[:, :, None] == jnp.arange(EXPERTS, dtype=jnp.int32)).astype(f32).sum(axis=1)
    order = jnp.arange(block, dtype=jnp.int32)
    before = (order[None, :] < order[:, None]).astype(bf16)
    earlier = jnp.dot(before, named.astype(bf16), preferred_element_type=f32).astype(jnp.int32)
    slot_of = jnp.where(named > 0, earlier, -1)
    picks = slot_of.T[:, None, :] == jnp.arange(CAP, dtype=jnp.int32)[None, :, None]
    pick_f32 = picks.astype(f32)
    pick = picks.astype(bf16).reshape(EXPERTS * CAP, block)

    def dispatch(part):
        rows = jnp.dot(pick, part, preferred_element_type=f32).astype(bf16)
        rows = lax.all_to_all(rows.reshape(EXPERTS, CAP, quarter), both, 0, 0, tiled=True)
        rows = lax.all_gather(rows, "tp", axis=2, tiled=True)
        return rows.reshape(EXPERTS * CAP, width)

    def bring_back(rows):
        rows = lax.psum_scatter(
            rows.reshape(EXPERTS, CAP, width), "tp", scatter_dimension=2, tiled=True
        )
        return combine(lax.all_to_all(rows, both, 0, 0, tiled=True))

    def combine(rows):
        rows = rows.reshape(EXPERTS * CAP, quarter)
        return lax.dot_general(pick, rows, (((0,), (0,)), ((), ())), preferred_element_type=f32)

    upstream_part = own_quarter(cotangent.reshape(block, width))
    up_rows = dispatch(upstream_part)
    upstream_part = upstream_part.astype(f32)

    flat_in = inputs.reshape(block, width).astype(f32)
    first_rms = inv_rms(flat_in)
    in_part = own_quarter(flat_in)
    normed_own = (flat_in * first_rms).astype(bf16)
    own_gains = lax.dynamic_slice_in_dim(qk_gains, ctx * HEAD_DIM, HEAD_DIM, axis=1).astype(f32)
    own_gains = own_gains[:, None, :]
    query_gain, key_gain = own_gains[0], own_gains[1]
    cosine, sine = signed_tables(0, length)
    (
        normed,
        head_weight,
        query_proj,
        key_proj,
        query_rot,
        key_rot,
        value_heads,
        qk_rms,
        attended,
        router_blocks,
    ) = attend(sizes, normed_own, qkv_scaled, own_gains, cosine, sine, router_own)
    normed = normed.reshape(length, width)
    head_weight = head_weight.reshape(width, 3 * HEAD_DIM)
    query_rms = qk_rms[:, :n_ctx].T.reshape(length, 1)
    key_rms = qk_rms[:, n_ctx:].T.reshape(length, 1)
    cosine, sine_table = rotary_tables(0, length)
    scores = attend_scores(query_rot, key_rot, scale, block)
    exponent = jnp.exp(scores - jnp.max(scores, axis=-1, keepdims=True))
    probs = exponent / jnp.sum(exponent, axis=-1, keepdims=True)
    probs_low = probs.astype(bf16)
    middle, small, chances, normed_mlp, rows, slot_gates = middle_stage(
        sizes, attended, out_all, in_part, router_blocks, pick.reshape(EXPERTS, CAP, block)
    )
    second_rms = small[EXPERTS][:, None]
    chances = chances.T
    per = places // n_tp
    router_part = lax.dynamic_slice_in_dim(router_blocks, tp * per, per, axis=0)
    router_part = router_part.transpose(0, 2, 1).reshape(quarter, EXPERTS)

    back_rows, slot_products, act_low, pre_grads, returned = expert_stage(
        sizes, rows, up_rows.reshape(places, CAP, width), expert_weight, slot_gates
    )
    rows = rows.reshape(EXPERTS * CAP, width)
    act_low = act_low.reshape(EXPERTS * CAP, hidden)
    pre_grads = pre_grads.reshape(EXPERTS * CAP, 2 * hidden)
    back_part = combine(back_rows)
    output_part = (middle + bring_back(returned)).astype(bf16)
    rows_in = (((0,), (0,)), ((), ()))
    expert_grads = jnp.concatenate(
        [
            lax.dot_general(rows, pre_grads, rows_in, preferred_element_type=f32),
            lax.dot_general(up_rows, act_low, rows_in, preferred_element_type=f32),
        ],
        axis=1,
    ).astype(bf16)
    expert_grads = lax.all_to_all(
        expert_grads.reshape(EXPERTS, depth, 3 * hidden), both, 0, 0, tiled=True
    ).astype(f32)
    slot_products = lax.psum(slot_products[:, 0, :CAP], "tp")

    chance_grads = jnp.sum(pick_f32 * slot_products[:, :, None], axis=1).T
    logit_grads = chances * (chance_grads - jnp.sum(chances * chance_grads, axis=-1, keepdims=True))
    scaled_mlp = back_part + jnp.dot(logit_grads, router_part.T, precision=highest)
    inner = lax.psum(jnp.sum(scaled_mlp * middle, axis=-1, keepdims=True), "tp")
    middle_grad = upstream_part + second_rms * scaled_mlp - middle * second_rms**3 / width * inner
    router_term = lax.dot_general(
        normed_mlp.astype(f32), logit_grads, rows_in, precision=highest
    )
    router_term = lax.all_gather(router_term, "tp", axis=0, tiled=True)
    router_term = lax.psum_scatter(router_term, both, scatter_dimension=0, tiled=True)
    grad_router = router_term * mlp_scale[:, None]

    branch_grad = lax.all_gather(middle_grad.astype(bf16), "tp", axis=1, tiled=True)
    grad_out = lax.dot_general(branch_grad, attended, rows_in, preferred_element_type=f32)
    grad_out = lax.psum_scatter(grad_out.astype(bf16), both, scatter_dimension=0, tiled=True)
    attended_grad = jnp.dot(branch_grad, out_all, preferred_element_type=f32).astype(bf16)
    attended_grad = attended_grad.reshape(block, n_ctx, HEAD_DIM).transpose(1, 0, 2)
    attended_grad = lax.all_to_all(attended_grad, "ctx", 0, 0, tiled=True)
    attended_grad = attended_grad.reshape(length, HEAD_DIM)
    prob_grads = jnp.einsum(
        "qd,kd->qk", attended_grad, value_heads, preferred_element_type=f32
    )
    score_grads = (
        probs * (prob_grads - jnp.sum(probs * prob_grads, axis=-1, keepdims=True))
    ).astype(bf16)
    query_grads = jnp.dot(score_grads, key_rot, preferred_element_type=f32) * scale
    key_grads = lax.dot_general(score_grads, query_rot, rows_in, preferred_element_type=f32) * scale
    value_grads = lax.dot_general(probs_low, attended_grad, rows_in, preferred_element_type=f32)
    query_norm_grad = rotate_back(query_grads, cosine, sine_table)
    key_norm_grad = rotate_back(key_grads, cosine, sine_table)
    query_scaled = query_norm_grad * query_gain
    key_scaled = key_norm_grad * key_gain
    inners = lax.psum(
        jnp.stack([jnp.sum(query_scaled * query_proj, axis=-1), jnp.sum(key_scaled * key_proj, axis=-1)]),
        ("ctx", "tp"),
    )
    query_pre = query_rms * query_scaled - query_proj * query_rms**3 / HQ * inners[0][:, None]
    key_pre = key_rms * key_scaled - key_proj * key_rms**3 / HQ * inners[1][:, None]
    gain_terms = jnp.stack(
        [
            jnp.sum(query_norm_grad * query_proj * query_rms, axis=0),
            jnp.sum(key_norm_grad * key_proj * key_rms, axis=0),
        ]
    )
    gain_terms = lax.all_gather(lax.psum(gain_terms, "fsdp"), "ctx", axis=1, tiled=True)
    proj_grads = jnp.concatenate([query_pre, key_pre, value_grads], axis=1).astype(bf16)
    qkv_grads = lax.dot_general(normed, proj_grads, rows_in, preferred_element_type=f32)
    qkv_grads = lax.all_to_all(
        qkv_grads.astype(bf16).reshape(places, depth, 3 * HEAD_DIM), both, 0, 0, tiled=True
    )
    qkv_grads = qkv_grads.astype(f32).reshape(n_fsdp, n_ctx, depth, 3 * HEAD_DIM).sum(axis=0)
    grad_qkv = (qkv_grads * attn_scale[None, :, None]).reshape(n_ctx, depth, 3, HEAD_DIM)
    grad_qkv = grad_qkv.transpose(1, 2, 0, 3).reshape(depth, 3, n_ctx * HEAD_DIM)
    scaled_first = lax.dot_general(
        proj_grads, head_weight, (((1,), (1,)), ((), ())), preferred_element_type=f32
    ).astype(bf16)
    scaled_first = lax.psum_scatter(scaled_first, "tp", scatter_dimension=1, tiled=True)
    scaled_first = lax.psum_scatter(scaled_first, "ctx", scatter_dimension=0, tiled=True)
    scaled_first = scaled_first.astype(f32)
    gains = jnp.stack(
        [
            jnp.sum(qkv_grads * qkv_raw, axis=(0, 2)),
            jnp.sum(expert_grads[:, :, : 2 * hidden] * gate_up_raw.astype(f32), axis=(0, 2)),
        ]
    )
    last_inner = jnp.sum(scaled_first * in_part, axis=-1)
    gains, last_inner = lax.psum((gains, last_inner), "tp")
    grad_mlp_gain = gains[1] + jnp.sum(router_term * router_f32, axis=-1)
    grad_inputs = (
        middle_grad
        + first_rms * scaled_first
        - in_part * first_rms**3 / width * last_inner[:, None]
    )
    grad_inputs = lax.all_gather(grad_inputs.astype(bf16), "tp", axis=1, tiled=True).astype(f32)
    output = lax.all_gather(output_part, "tp", axis=1, tiled=True)
    grad_gate_up = (expert_grads[:, :, : 2 * hidden] * mlp_scale[None, :, None]).reshape(
        EXPERTS, depth, 2, hidden
    )
    return (
        output[None],
        grad_inputs[None],
        gains[0],
        grad_qkv,
        grad_out.astype(f32),
        gain_terms,
        grad_mlp_gain,
        grad_router,
        grad_gate_up.transpose(1, 2, 0, 3),
        expert_grads[:, :, 2 * hidden :].transpose(1, 0, 2),
    )


def solution(mesh):
    sizes = (mesh.shape["fsdp"], mesh.shape["ctx"], mesh.shape["tp"])
    one_expert = sizes[0] * sizes[1] == EXPERTS
    one_head = sizes[1] * sizes[2] * HEAD_DIM == HQ

    def step(*arrays):
        if one_expert and one_head and arrays[0].shape[0] == 1:
            return by_head(sizes, *arrays)
        return on_device(*arrays)

    placed = (
        P("fsdp", "ctx", None),
        P(("fsdp", "ctx")),
        P(("fsdp", "ctx"), None, "tp"),
        P(("fsdp", "ctx"), "tp"),
        P(None, "tp"),
        P(("fsdp", "ctx")),
        P(("fsdp", "ctx"), None),
        P(("fsdp", "ctx"), None, None, "tp"),
        P(("fsdp", "ctx"), None, "tp"),
        P("ctx", "fsdp", None, None),
        P("fsdp", "ctx", None),
    )
    return jax.shard_map(
        step,
        mesh=mesh,
        in_specs=placed,
        out_specs=(
            P("fsdp", "ctx", None),
            P("fsdp", "ctx", None),
            P(("fsdp", "ctx")),
            P(("fsdp", "ctx"), None, "tp"),
            P(("fsdp", "ctx"), "tp"),
            P(None, "tp"),
            P(("fsdp", "ctx")),
            P(("fsdp", "ctx"), None),
            P(("fsdp", "ctx"), None, None, "tp"),
            P(("fsdp", "ctx"), None, "tp"),
        ),
        check_vma=False,
    )
```

```python
import functools
import math

import jax
import jax.numpy as jnp
from jax import lax
from jax.experimental import pallas as pl
from jax.experimental.pallas import tpu as pltpu
from jax.sharding import PartitionSpec as P

HEAD_DIM = 128
TOPK = 4
EXPERTS = 8
HQ = 2048
CAP = 160


epsilon = 1e-05
highest = lax.Precision.HIGHEST


def inv_rms(values):
    return lax.rsqrt(jnp.mean(values * values, axis=-1, keepdims=True) + epsilon)


def rotary_tables(offset, length):
    half_dim = HEAD_DIM // 2
    frequency = jnp.exp(
        jnp.arange(half_dim, dtype=jnp.float32) * (-2.0 * math.log(10000.0) / HEAD_DIM)
    )
    positions = (offset + jnp.arange(length, dtype=jnp.int32)).astype(jnp.float32)
    angles = positions[:, None] * frequency[None, :]
    angles = jnp.concatenate([angles, angles], axis=1)
    return (jnp.cos(angles), jnp.sin(angles))


def rotate(values, cosine, sine_table):
    half_dim = values.shape[-1] // 2
    turned = jnp.concatenate([-values[..., half_dim:], values[..., :half_dim]], axis=-1)
    return values * cosine + turned * sine_table


def rotate_back(grads, cosine, sine_table):
    half_dim = grads.shape[-1] // 2
    scaled = grads * sine_table
    return grads * cosine + jnp.concatenate(
        [scaled[..., half_dim:], -scaled[..., :half_dim]], axis=-1
    )


def slot_table(routed):
    flat_routes = routed.reshape(-1)
    one_hot = (flat_routes[:, None] == jnp.arange(EXPERTS, dtype=jnp.int32)[None, :]).astype(
        jnp.int32
    )
    earlier = jnp.cumsum(one_hot, axis=0) - one_hot
    within = jnp.sum(earlier * one_hot, axis=1)
    slots = flat_routes * CAP + within
    owners = jnp.arange(flat_routes.shape[0], dtype=jnp.int32) // TOPK
    token_of = jnp.zeros((EXPERTS * CAP,), jnp.int32).at[slots].set(owners)
    filled = jnp.zeros((EXPERTS * CAP,), jnp.float32).at[slots].set(1.0)
    return (slots.reshape(routed.shape), token_of, filled)


def on_device(
    inputs,
    attn_gain,
    qkv_weight,
    out_weight,
    qk_gains,
    mlp_gain,
    router_weight,
    gate_up_weight,
    down_weight,
    routes,
    cotangent,
):
    seq_dev, block, width = inputs.shape
    rows = seq_dev * block
    heads_dev = qkv_weight.shape[2] // HEAD_DIM
    scale = 1.0 / math.sqrt(HEAD_DIM)
    place = lax.axis_index("ctx")
    attn_gain_all, qkv_all, out_all, mlp_gain_all, router_all = (
        lax.all_gather(attn_gain, ("fsdp", "ctx"), axis=0, tiled=True),
        lax.all_gather(qkv_weight, ("fsdp", "ctx"), axis=0, tiled=True),
        lax.all_gather(out_weight, ("fsdp", "ctx"), axis=0, tiled=True),
        lax.all_gather(mlp_gain, ("fsdp", "ctx"), axis=0, tiled=True),
        lax.all_gather(router_weight, ("fsdp", "ctx"), axis=0, tiled=True),
    )
    attn_scale = attn_gain_all.astype(jnp.float32)
    mlp_scale = mlp_gain_all.astype(jnp.float32)
    flat_in = inputs.reshape(rows, width).astype(jnp.float32)
    first_rms = inv_rms(flat_in)
    normed = (flat_in * first_rms * attn_scale).astype(jnp.bfloat16)
    projected = jnp.einsum("td,dch->tch", normed, qkv_all, preferred_element_type=jnp.float32)
    query_proj = projected[:, 0]
    key_proj = projected[:, 1]
    query_sums, key_sums = lax.psum(
        (jnp.sum(query_proj * query_proj, axis=-1), jnp.sum(key_proj * key_proj, axis=-1)), "tp"
    )
    query_rms = lax.rsqrt(query_sums / HQ + epsilon)[:, None]
    key_rms = lax.rsqrt(key_sums / HQ + epsilon)[:, None]
    query_gain = qk_gains[0].astype(jnp.float32)
    key_gain = qk_gains[1].astype(jnp.float32)
    query_norm = query_proj * query_rms * query_gain
    key_norm = key_proj * key_rms * key_gain
    cosine, sine_table = rotary_tables(place * block, block)
    cos_heads = cosine[:, None, :]
    sin_heads = sine_table[:, None, :]
    head_shape = (seq_dev, block, heads_dev, HEAD_DIM)
    query_rot = rotate(query_norm.reshape(head_shape), cos_heads, sin_heads).astype(jnp.bfloat16)
    key_rot = rotate(key_norm.reshape(head_shape), cos_heads, sin_heads).astype(jnp.bfloat16)
    value_heads = projected[:, 2].reshape(head_shape).astype(jnp.bfloat16)
    key_all, value_all = (
        lax.all_gather(key_rot, "ctx", axis=1, tiled=True),
        lax.all_gather(value_heads, "ctx", axis=1, tiled=True),
    )
    length = key_all.shape[1]
    key_block = jnp.arange(length, dtype=jnp.int32) // block
    allowed = (key_block <= place)[None, None, None, :]
    scores = (
        jnp.einsum("sqhd,skhd->shqk", query_rot, key_all, preferred_element_type=jnp.float32)
        * scale
    )
    scores = jnp.where(allowed, scores, -1e30)
    top_score = jnp.max(scores, axis=-1, keepdims=True)
    exponent = jnp.exp(scores - top_score)
    total = jnp.sum(exponent, axis=-1, keepdims=True)
    log_total = top_score + jnp.log(total)
    softmaxed = exponent / total
    attended = jnp.einsum(
        "shqk,skhd->sqhd",
        softmaxed.astype(jnp.bfloat16),
        value_all,
        preferred_element_type=jnp.float32,
    )
    attended = attended.reshape(rows, heads_dev * HEAD_DIM).astype(jnp.bfloat16)
    branch = lax.psum(
        jnp.einsum("th,dh->td", attended, out_all, preferred_element_type=jnp.float32), "tp"
    )
    middle = flat_in + branch
    second_rms = inv_rms(middle)
    normed_mlp = (middle * second_rms * mlp_scale).astype(jnp.bfloat16)
    logits = jnp.dot(normed_mlp, router_all, preferred_element_type=jnp.float32)
    chances = jax.nn.softmax(logits, axis=-1)
    routed = routes.reshape(rows, TOPK)
    gates = jnp.take_along_axis(chances, routed, axis=-1)
    slots, token_of, filled = slot_table(routed)
    dispatched = (normed_mlp[token_of] * filled[:, None].astype(jnp.bfloat16)).reshape(
        EXPERTS, CAP, width
    )
    gate_up_all, down_all = (
        lax.all_gather(gate_up_weight, ("fsdp", "ctx"), axis=0, tiled=True),
        lax.all_gather(down_weight, ("fsdp", "ctx"), axis=0, tiled=True),
    )
    gate_up = jnp.einsum(
        "ecd,djef->ecjf", dispatched, gate_up_all, preferred_element_type=jnp.float32
    )
    gate_part = gate_up[:, :, 0]
    up_part = gate_up[:, :, 1]
    activated = (jax.nn.silu(gate_part) * up_part).astype(jnp.bfloat16)
    upstream = cotangent.reshape(rows, width).astype(jnp.float32)
    slot_gates = (
        jnp.zeros((EXPERTS * CAP,), jnp.float32)
        .at[slots.reshape(-1)]
        .set(gates.reshape(-1))
        .reshape(EXPERTS, CAP)
    )
    token_grid = token_of.reshape(EXPERTS, CAP)
    filled_grid = filled.reshape(EXPERTS, CAP)

    def expert_forward(expert_index, running):
        combined, slot_products = running
        expert_down = lax.dynamic_index_in_dim(down_all, expert_index, 1, keepdims=False)
        expert_act = lax.dynamic_index_in_dim(activated, expert_index, 0, keepdims=False)
        expert_tokens = lax.dynamic_index_in_dim(token_grid, expert_index, 0, keepdims=False)
        expert_gates = lax.dynamic_index_in_dim(slot_gates, expert_index, 0, keepdims=False)
        returned_rows = jnp.einsum(
            "cf,df->cd", expert_act, expert_down, preferred_element_type=jnp.float32
        )
        combined = combined.at[expert_tokens].add(returned_rows * expert_gates[:, None])
        products = jnp.sum(returned_rows * upstream[expert_tokens], axis=-1)
        slot_products = lax.dynamic_update_index_in_dim(slot_products, products, expert_index, 0)
        return (combined, slot_products)

    combined, slot_products = lax.fori_loop(
        0,
        EXPERTS,
        expert_forward,
        (jnp.zeros((rows, width), jnp.float32), jnp.zeros((EXPERTS, CAP), jnp.float32)),
    )
    gate_grad_part = slot_products.reshape(-1)[slots]
    expert_sum = lax.psum(combined, "tp")
    output = (middle + expert_sum).astype(jnp.bfloat16).reshape(seq_dev, block, width)
    slot_grads = (
        (slot_gates.reshape(-1)[:, None] * upstream[token_of])
        .astype(jnp.bfloat16)
        .reshape(EXPERTS, CAP, width)
    )
    gate_up_back, down_back = (
        lax.all_gather(gate_up_weight, ("fsdp", "ctx"), axis=0, tiled=True),
        lax.all_gather(down_weight, ("fsdp", "ctx"), axis=0, tiled=True),
    )
    act_grads = jnp.einsum(
        "ecd,def->ecf", slot_grads, down_back, preferred_element_type=jnp.float32
    )
    sigmoid = jax.nn.sigmoid(gate_part)
    gate_grads = act_grads * up_part * sigmoid * (1.0 + gate_part * (1.0 - sigmoid))
    up_grads = act_grads * (gate_part * sigmoid)
    pre_grads = jnp.stack([gate_grads, up_grads], axis=2).astype(jnp.bfloat16)

    def expert_backward(expert_index, running):
        expert_pre = lax.dynamic_index_in_dim(pre_grads, expert_index, 0, keepdims=False)
        expert_weight = lax.dynamic_index_in_dim(gate_up_back, expert_index, 2, keepdims=False)
        expert_tokens = lax.dynamic_index_in_dim(token_grid, expert_index, 0, keepdims=False)
        expert_filled = lax.dynamic_index_in_dim(filled_grid, expert_index, 0, keepdims=False)
        expert_back = jnp.einsum(
            "cjf,djf->cd", expert_pre, expert_weight, preferred_element_type=jnp.float32
        )
        return running.at[expert_tokens].add(expert_back * expert_filled[:, None])

    expert_input_part = lax.fori_loop(
        0, EXPERTS, expert_backward, jnp.zeros((rows, width), jnp.float32)
    )
    gate_up_term = jnp.einsum(
        "ecd,ecjf->djef", dispatched, pre_grads, preferred_element_type=jnp.float32
    )
    down_term = jnp.einsum(
        "ecf,ecd->def", activated, slot_grads, preferred_element_type=jnp.float32
    )
    expert_grads = lax.psum_scatter(
        jnp.concatenate([gate_up_term, down_term[:, None]], axis=1),
        ("fsdp", "ctx"),
        scatter_dimension=0,
        tiled=True,
    )
    gate_up_share = expert_grads[:, :2]
    down_share = expert_grads[:, 2]
    expert_input, gate_total = lax.psum((expert_input_part, gate_grad_part), "tp")
    chosen = (routed[:, :, None] == jnp.arange(EXPERTS, dtype=jnp.int32)[None, None, :]).astype(
        jnp.float32
    )
    chance_grads = jnp.sum(gate_total[:, :, None] * chosen, axis=1)
    logit_grads = chances * (chance_grads - jnp.sum(chances * chance_grads, axis=-1, keepdims=True))
    router_f32 = router_all.astype(jnp.float32)
    mlp_input = expert_input + jnp.dot(logit_grads, router_f32.T, precision=highest)
    grad_router = jnp.dot(normed_mlp.astype(jnp.float32).T, logit_grads, precision=highest)
    grad_mlp_gain = jnp.sum(mlp_input * middle * second_rms, axis=0)
    scaled_mlp = mlp_input * mlp_scale
    middle_grad = (
        upstream
        + second_rms * scaled_mlp
        - middle * second_rms**3 / width * jnp.sum(scaled_mlp * middle, axis=-1, keepdims=True)
    )
    branch_grad = middle_grad.astype(jnp.bfloat16)
    grad_out = jnp.einsum("td,th->dh", branch_grad, attended, preferred_element_type=jnp.float32)
    attended_grad = (
        jnp.dot(branch_grad, out_all, preferred_element_type=jnp.float32)
        .astype(jnp.bfloat16)
        .reshape(head_shape)
    )
    again_scores = (
        jnp.einsum("sqhd,skhd->shqk", query_rot, key_all, preferred_element_type=jnp.float32)
        * scale
    )
    again_scores = jnp.where(allowed, again_scores, -1e30)
    recomputed = jnp.exp(again_scores - log_total)
    prob_grads = jnp.einsum(
        "sqhd,skhd->shqk", attended_grad, value_all, preferred_element_type=jnp.float32
    )
    score_grads = (
        recomputed * (prob_grads - jnp.sum(recomputed * prob_grads, axis=-1, keepdims=True))
    ).astype(jnp.bfloat16)
    query_grads = (
        jnp.einsum("shqk,skhd->sqhd", score_grads, key_all, preferred_element_type=jnp.float32)
        * scale
    )
    key_grads = (
        jnp.einsum("shqk,sqhd->skhd", score_grads, query_rot, preferred_element_type=jnp.float32)
        * scale
    )
    value_grads = jnp.einsum(
        "shqk,sqhd->skhd",
        recomputed.astype(jnp.bfloat16),
        attended_grad,
        preferred_element_type=jnp.float32,
    )
    key_back, value_back = (
        lax.psum_scatter(key_grads, "ctx", scatter_dimension=1, tiled=True),
        lax.psum_scatter(value_grads, "ctx", scatter_dimension=1, tiled=True),
    )
    query_norm_grad = rotate_back(query_grads, cos_heads, sin_heads).reshape(rows, -1)
    key_norm_grad = rotate_back(key_back, cos_heads, sin_heads).reshape(rows, -1)
    query_scaled = query_norm_grad * query_gain
    key_scaled = key_norm_grad * key_gain
    query_inner, key_inner = lax.psum(
        (jnp.sum(query_scaled * query_proj, axis=-1), jnp.sum(key_scaled * key_proj, axis=-1)), "tp"
    )
    query_pre = query_rms * query_scaled - query_proj * query_rms**3 / HQ * query_inner[:, None]
    key_pre = key_rms * key_scaled - key_proj * key_rms**3 / HQ * key_inner[:, None]
    gain_terms = jnp.stack(
        [
            jnp.sum(query_norm_grad * query_proj * query_rms, axis=0),
            jnp.sum(key_norm_grad * key_proj * key_rms, axis=0),
        ]
    )
    grad_qk_gains = lax.psum(gain_terms, ("fsdp", "ctx"))
    proj_grads = jnp.stack([query_pre, key_pre, value_back.reshape(rows, -1)], axis=1).astype(
        jnp.bfloat16
    )
    grad_qkv = jnp.einsum("td,tch->dch", normed, proj_grads, preferred_element_type=jnp.float32)
    normed_grad = lax.psum(
        jnp.einsum("tch,dch->td", proj_grads, qkv_all, preferred_element_type=jnp.float32), "tp"
    )
    grad_attn_gain = jnp.sum(normed_grad * flat_in * first_rms, axis=0)
    scaled_first = normed_grad * attn_scale
    grad_inputs = (
        middle_grad
        + first_rms * scaled_first
        - flat_in * first_rms**3 / width * jnp.sum(scaled_first * flat_in, axis=-1, keepdims=True)
    )
    shares = (
        lax.psum_scatter(grad_attn_gain, ("fsdp", "ctx"), scatter_dimension=0, tiled=True),
        lax.psum_scatter(grad_qkv, ("fsdp", "ctx"), scatter_dimension=0, tiled=True),
        lax.psum_scatter(grad_out, ("fsdp", "ctx"), scatter_dimension=0, tiled=True),
        lax.psum_scatter(grad_mlp_gain, ("fsdp", "ctx"), scatter_dimension=0, tiled=True),
        lax.psum_scatter(grad_router, ("fsdp", "ctx"), scatter_dimension=0, tiled=True),
    )
    return (
        output,
        grad_inputs.reshape(seq_dev, block, width),
        shares[0],
        shares[1],
        shares[2],
        grad_qk_gains,
        shares[3],
        shares[4],
        gate_up_share,
        down_share,
    )


MESH = pl.DeviceIdType.MESH


def remote(src, dst, send, recv, **where):
    return pltpu.make_async_remote_copy(
        src_ref=src, dst_ref=dst, send_sem=send, recv_sem=recv, device_id=where, device_id_type=MESH
    )


def greet(peers):
    barrier = pltpu.get_barrier_semaphore()
    for where in peers:
        pl.semaphore_signal(barrier, inc=1, device_id=where, device_id_type=MESH)
    pl.semaphore_wait(barrier, len(peers))


def in_group(sizes, step):
    _, n_ctx, n_tp = sizes
    here = lax.axis_index("ctx") * n_tp + lax.axis_index("tp")
    there = lax.rem(here + step, n_ctx * n_tp)
    return {"ctx": there // n_tp, "tp": lax.rem(there, n_tp)}, there


def rows_at(place, size):
    return pl.ds(pl.multiple_of(place * size, size), size)


def dot_f32(a, b, dims, precision=None):
    return lax.dot_general(
        a, b, (dims, ((), ())), precision=precision, preferred_element_type=jnp.float32
    )


def group_sum(sizes, own, parts, send, recv):
    _, n_ctx, n_tp = sizes
    others = n_ctx * n_tp - 1
    here = lax.axis_index("ctx") * n_tp + lax.axis_index("tp")
    copies = []
    for step in range(1, others + 1):
        where, _ = in_group(sizes, step)
        copies.append(remote(own, parts.at[here], send.at[step - 1], recv.at[step - 1], **where))
        copies[-1].start()
    total = own[...]
    for step in range(1, others + 1):
        copies[step - 1].wait_recv()
        _, there = in_group(sizes, others + 1 - step)
        total = total + parts[there]
    for copy in copies:
        copy.wait_send()
    return total


def attend_kernel(
    sizes,
    scale,
    own_rows,
    weight,
    gains,
    cosine,
    sine,
    own_router,
    normed,
    head_weight,
    query_proj,
    key_proj,
    query_rot,
    key_rot,
    value,
    rms,
    attended,
    router,
    own_attended,
    own_sums,
    sums,
    w_send,
    w_recv,
    x_send,
    x_recv,
    n_send,
    n_recv,
    y_send,
    y_recv,
    c_send,
    c_recv,
    s_send,
    s_recv,
    a_send,
    a_recv,
    r_send,
    r_recv,
):
    n_fsdp, n_ctx, n_tp = sizes
    fsdp, ctx, tp = lax.axis_index("fsdp"), lax.axis_index("ctx"), lax.axis_index("tp")
    block = own_rows.shape[0]
    share = block // n_tp
    half_dim = HEAD_DIM // 2
    mate = tp + 1 - 2 * lax.rem(tp, 2)
    over = lax.rem(tp + 2, n_tp)
    over_mate = lax.rem(mate + 2, n_tp)
    across = 1 - fsdp
    places = n_fsdp * n_ctx
    me = fsdp * n_ctx + ctx
    greet(
        [in_group(sizes, step)[0] for step in range(1, n_ctx * n_tp)]
        + [
            {"fsdp": across, "ctx": lax.rem(ctx + step, n_ctx)}
            for step in range(n_ctx)
        ]
    )

    copies = []

    def go(*args, **where):
        copy = remote(*args, **where)
        copy.start()
        copies.append(copy)
        return copy

    def back(step):
        return lax.rem(ctx + n_ctx - step, n_ctx)

    mine = rows_at(tp, share)
    from_w, from_n, from_y, from_c, from_x = {}, {}, {}, {}, {}
    for step in range(1, n_ctx):
        there = lax.rem(ctx + step, n_ctx)
        from_w[step] = go(
            weight.at[there],
            head_weight.at[fsdp * n_ctx + ctx],
            w_send.at[step - 1],
            w_recv.at[step - 1],
            ctx=there,
        )
    from_x[0] = go(
        weight.at[ctx],
        head_weight.at[fsdp * n_ctx + ctx],
        x_send.at[0],
        x_recv.at[0],
        fsdp=across,
    )
    for step in range(1, n_ctx):
        there = lax.rem(ctx + step, n_ctx)
        from_n[step] = go(
            own_rows.at[mine], normed.at[ctx, mine], n_send.at[step - 1], n_recv.at[step - 1], ctx=there
        )
    from_r = []
    for step in range(1, places):
        there = later(sizes, step)
        from_r.append(
            go(
                own_router,
                router.at[me],
                r_send.at[step - 1],
                r_recv.at[step - 1],
                **place_at(sizes, there),
            )
        )
    router[me] = own_router[...]
    head_weight[fsdp * n_ctx + ctx] = weight[ctx]
    normed[ctx] = own_rows[...]
    for step in range(1, n_ctx):
        origin = back(step)
        from_w[step].wait_recv()
        piece = head_weight.at[fsdp * n_ctx + origin]
        from_x[step] = go(piece, piece, x_send.at[step], x_recv.at[step], fsdp=across)
        from_n[step].wait_recv()
        piece = normed.at[origin, mine]
        from_y[step] = go(piece, piece, y_send.at[step - 1], y_recv.at[step - 1], tp=over)
        from_c[step, 0] = go(
            piece, piece, c_send.at[step - 1, 0], c_recv.at[step - 1, 0], tp=mate
        )
    for step in range(1, n_ctx):
        from_y[step].wait_recv()
        piece = normed.at[back(step), rows_at(over, share)]
        from_c[step, 1] = go(
            piece, piece, c_send.at[step - 1, 1], c_recv.at[step - 1, 1], tp=mate
        )
    for step in range(n_ctx):
        from_x[step].wait_recv()

    width = head_weight.shape[0] * head_weight.shape[1]
    line = lax.broadcasted_iota(jnp.int32, own_sums.shape, 0)
    ones = jnp.ones((2 * n_ctx, HEAD_DIM), jnp.float32)
    all_sums = jnp.zeros(own_sums.shape, jnp.float32)
    for step in range(n_ctx):
        if step:
            from_c[step, 0].wait_recv()
            from_c[step, 1].wait_recv()
        origin = back(step)
        here = rows_at(origin, block)
        projected = dot_f32(
            normed[origin], head_weight[...].reshape(width, 3 * HEAD_DIM), ((1,), (0,))
        )
        query, key = projected[:, :HEAD_DIM], projected[:, HEAD_DIM : 2 * HEAD_DIM]
        query_proj[here] = query
        key_proj[here] = key
        value[here] = projected[:, 2 * HEAD_DIM :].astype(value.dtype)
        query_sum = dot_f32(ones, query * query, ((1,), (1,)), highest)
        key_sum = dot_f32(ones, key * key, ((1,), (1,)), highest)
        all_sums = jnp.where(line == origin, query_sum, all_sums)
        all_sums = jnp.where(line == origin + n_ctx, key_sum, all_sums)
    own_sums[...] = all_sums
    total = group_sum(sizes, own_sums, sums, s_send, s_recv)
    inverse = lax.rsqrt(total / HQ + epsilon)
    columns = inverse.T
    rms[...] = columns
    for place in range(n_ctx):
        here = slice(place * block, (place + 1) * block)
        cos_here, sin_here = cosine[here], sine[here]
        for proj, rot, which in ((query_proj, query_rot, 0), (key_proj, key_rot, 1)):
            scaled = proj[here] * columns[:, which * n_ctx + place][:, None] * gains[which]
            turned = pltpu.roll(scaled, half_dim, 1)
            rot[here] = (scaled * cos_here + turned * sin_here).astype(rot.dtype)
    from_a = {}
    for place in range(n_ctx):
        here = slice(place * block, (place + 1) * block)
        seen = slice(0, (place + 1) * block)
        scores = dot_f32(query_rot[here], key_rot[seen], ((1,), (1,))) * scale
        exponent = jnp.exp(scores - jnp.max(scores, axis=-1, keepdims=True))
        probs = exponent / jnp.sum(exponent, axis=-1, keepdims=True)
        mixed = dot_f32(probs.astype(value.dtype), value[seen], ((1,), (0,)))
        own_attended[place] = mixed.astype(own_attended.dtype)
        lanes = rows_at(ctx, HEAD_DIM)
        from_a[place] = remote(
            own_attended.at[place],
            attended.at[:, lanes],
            a_send.at[place],
            a_recv.at[ctx],
            ctx=place,
        )

        @pl.when(ctx != place)
        def _():
            from_a[place].start()

        @pl.when(ctx == place)
        def _():
            attended[:, lanes] = own_attended[place]

    for place in range(n_ctx):

        @pl.when(ctx != place)
        def _():
            from_a[place].wait_send()
            remote(
                own_attended.at[place],
                attended.at[:, rows_at(place, HEAD_DIM)],
                a_send.at[place],
                a_recv.at[place],
                ctx=place,
            ).wait_recv()

    for copy in from_r:
        copy.wait_recv()
    for copy in copies:
        copy.wait_send()


def attend(sizes, own_rows, weight, gains, cosine, sine, router):
    n_fsdp, n_ctx, n_tp = sizes
    block, width = own_rows.shape
    _, depth, columns = weight.shape
    length = n_ctx * block
    group = n_ctx * n_tp
    bf16, f32 = jnp.bfloat16, jnp.float32
    vmem = pl.BlockSpec(memory_space=pltpu.VMEM)
    dma = pltpu.SemaphoreType.DMA
    shape = jax.ShapeDtypeStruct
    outs = (
        shape((n_ctx, block, width), bf16),
        shape((n_fsdp * n_ctx, depth, columns), bf16),
        shape((length, HEAD_DIM), f32),
        shape((length, HEAD_DIM), f32),
        shape((length, HEAD_DIM), bf16),
        shape((length, HEAD_DIM), bf16),
        shape((length, HEAD_DIM), bf16),
        shape((block, 2 * n_ctx), f32),
        shape((block, n_ctx * HEAD_DIM), bf16),
        shape((n_fsdp * n_ctx,) + router.shape, f32),
    )
    pairs = [
        (n_ctx - 1,),
        (n_ctx,),
        (n_ctx - 1,),
        (n_ctx - 1,),
        (n_ctx - 1, 2),
        (group - 1,),
        (n_ctx,),
        (n_fsdp * n_ctx - 1,),
    ]
    return pl.pallas_call(
        functools.partial(attend_kernel, sizes, 1.0 / math.sqrt(HEAD_DIM)),
        name="attend",
        out_shape=outs,
        in_specs=[vmem] * 6,
        out_specs=(vmem,) * len(outs),
        scratch_shapes=[
            pltpu.VMEM((n_ctx, block, HEAD_DIM), bf16),
            pltpu.VMEM((2 * n_ctx, block), f32),
            pltpu.VMEM((group, 2 * n_ctx, block), f32),
        ]
        + [dma(size) for size in pairs for _ in range(2)],
        compiler_params=pltpu.CompilerParams(collective_id=0, has_side_effects=True),
        cost_estimate=pl.CostEstimate(
            flops=70_000_000_000, bytes_accessed=20_000_000, transcendentals=1_000_000
        ),
    )(own_rows, weight, gains, cosine, sine, router)


def signed_tables(offset, length):
    cosine, sine = rotary_tables(offset, length)
    half_dim = HEAD_DIM // 2
    return cosine, jnp.concatenate([-sine[:, :half_dim], sine[:, half_dim:]], axis=1)


def around(sizes):
    n_fsdp, n_ctx, n_tp = sizes
    me = lax.axis_index("fsdp") * n_ctx + lax.axis_index("ctx")
    tp = lax.axis_index("tp")
    mate = tp + 1 - 2 * lax.rem(tp, 2)
    over = lax.rem(tp + 2, n_tp)
    return me, tp, mate, over, lax.rem(mate + 2, n_tp)


def place_at(sizes, place):
    return {"fsdp": place // sizes[1], "ctx": lax.rem(place, sizes[1])}


def later(sizes, step):
    places = sizes[0] * sizes[1]
    me = lax.axis_index("fsdp") * sizes[1] + lax.axis_index("ctx")
    return lax.rem(me + step, places)


def tp_sum(own, parts, send, recv, peers):
    copies = [
        remote(own, parts.at[i], send.at[i], recv.at[i], tp=peer) for i, peer in enumerate(peers)
    ]
    for copy in copies:
        copy.start()
    total = own[...]
    for i, copy in enumerate(copies):
        copy.wait_recv()
        total = total + parts[i]
    for copy in copies:
        copy.wait_send()
    return total


def middle_kernel(
    sizes,
    attended,
    out_all,
    in_part,
    router,
    pick,
    middle,
    small,
    chances,
    normed,
    rows,
    gates,
    c_out,
    c_in,
    y_out,
    y_in,
    own_small,
    smalls,
    rows_out,
    gates_out,
    m_send,
    m_recv,
    t_send,
    t_recv,
    z_send,
    z_recv,
    g_send,
    g_recv,
    y_send,
    y_recv,
    c_send,
    c_recv,
    d_send,
    d_recv,
):
    bf16, f32 = jnp.bfloat16, jnp.float32
    n_fsdp, n_ctx, n_tp = sizes
    places = n_fsdp * n_ctx
    me, tp, mate, over, over_mate = around(sizes)
    quarter = in_part.shape[1]
    width = quarter * n_tp
    per = places // n_tp
    greet(
        [{"tp": peer} for peer in (mate, over, over_mate)]
        + [place_at(sizes, later(sizes, step)) for step in range(1, places)]
    )

    def branch(which):
        return dot_f32(attended[...], out_all[rows_at(which, quarter)], ((1,), (1,)))

    to_mate = []
    for i, which in enumerate((over_mate, mate)):
        c_out[i] = branch(which).astype(bf16)
        to_mate.append(remote(c_out.at[i], c_in.at[i], m_send.at[i], m_recv.at[i], tp=mate))
        to_mate[i].start()
    part = branch(over)
    to_mate[0].wait_recv()
    y_out[...] = (part + c_in[0].astype(f32)).astype(bf16)
    to_over = remote(y_out, y_in, m_send.at[2], m_recv.at[2], tp=over)
    to_over.start()
    part = in_part[...] + branch(tp)
    to_mate[1].wait_recv()
    part = part + c_in[1].astype(f32)
    to_over.wait_recv()
    part = part + y_in[...].astype(f32)
    for copy in (*to_mate, to_over):
        copy.wait_send()
    middle[...] = part

    depth = quarter // per
    raw = jnp.zeros((EXPERTS, part.shape[0]), f32)
    for i in range(per):
        raw = raw + dot_f32(
            router[tp * per + i], part[:, i * depth : (i + 1) * depth], ((1,), (1,)), highest
        )
    own_small[:EXPERTS] = raw
    own_small[EXPERTS:] = dot_f32(jnp.ones((8, quarter), f32), part * part, ((1,), (1,)), highest)
    total = tp_sum(own_small, smalls, t_send, t_recv, (mate, over, over_mate))
    inverse = lax.rsqrt(total[EXPERTS:] / width + epsilon)
    small[:EXPERTS] = total[:EXPERTS]
    small[EXPERTS:] = inverse
    logits = total[:EXPERTS] * inverse[:1]
    exponent = jnp.exp(logits - jnp.max(logits, axis=0, keepdims=True))
    chances[...] = exponent / jnp.sum(exponent, axis=0, keepdims=True)
    normed[...] = (part * inverse.T[:, :1]).astype(bf16)

    lanes = rows_at(tp, quarter)
    over_lanes = rows_at(over, quarter)

    def own_row(step):
        return remote(
            rows_out.at[later(sizes, step)],
            rows.at[me, :, lanes],
            z_send.at[step],
            z_recv.at[step],
            **place_at(sizes, later(sizes, step)),
        )

    def own_gate(step):
        return remote(
            gates_out.at[later(sizes, step)],
            gates.at[me],
            g_send.at[step],
            g_recv.at[step],
            **place_at(sizes, later(sizes, step)),
        )

    def onward(step, which, send, recv, peer):
        piece = rows.at[later(sizes, places - step), :, which]
        return remote(piece, piece, send.at[step], recv.at[step], tp=peer)

    def to_y(step):
        return onward(step, lanes, y_send, y_recv, over)

    def to_c(step):
        return onward(step, lanes, c_send, c_recv, mate)

    def to_d(step):
        return onward(step, over_lanes, d_send, d_recv, mate)

    def build(step, carry):
        there = later(sizes, step)
        rows_out[there] = dot_f32(pick[there], normed[...], ((1,), (0,))).astype(bf16)
        chance = jnp.broadcast_to(chances[pl.ds(there, 1)], (8, chances.shape[1]))
        gates_out[there, :, :CAP] = dot_f32(
            chance, pick[there].astype(f32), ((1,), (1,)), highest
        )

        @pl.when(step < places)
        def _():
            own_row(step).start()
            own_gate(step).start()

        return carry

    gates_out[...] = jnp.zeros_like(gates_out)
    lax.fori_loop(1, places + 1, build, 0)
    rows[me, :, lanes] = rows_out[me]
    gates[me] = gates_out[me]
    to_y(0).start()
    to_c(0).start()

    def pass_on(step, carry):
        own_row(step).wait_recv()
        to_y(step).start()
        to_c(step).start()
        to_y(step - 1).wait_recv()
        to_d(step - 1).start()
        return carry

    lax.fori_loop(1, places, pass_on, 0)
    to_y(places - 1).wait_recv()
    to_d(places - 1).start()

    def finish(step, carry):
        to_c(step).wait_recv()
        to_d(step).wait_recv()
        to_c(step).wait_send()
        to_d(step).wait_send()
        to_y(step).wait_send()

        @pl.when(step > 0)
        def _():
            own_row(step).wait_send()
            own_gate(step).wait()

        return carry

    lax.fori_loop(0, places, finish, 0)


def middle_stage(sizes, attended, out_all, in_part, router, pick):
    n_fsdp, n_ctx, n_tp = sizes
    places = n_fsdp * n_ctx
    block, quarter = in_part.shape
    bf16, f32 = jnp.bfloat16, jnp.float32
    vmem = pl.BlockSpec(memory_space=pltpu.VMEM)
    dma = pltpu.SemaphoreType.DMA
    shape = jax.ShapeDtypeStruct
    outs = (
        shape((block, quarter), f32),
        shape((EXPERTS + 8, block), f32),
        shape((EXPERTS, block), f32),
        shape((block, quarter), bf16),
        shape((places, CAP, quarter * n_tp), bf16),
        shape((places, 8, block), f32),
    )
    pairs = [3, 3, places, places, places, places, places]
    return pl.pallas_call(
        functools.partial(middle_kernel, sizes),
        name="middle",
        out_shape=outs,
        in_specs=[vmem] * 5,
        out_specs=(vmem,) * len(outs),
        scratch_shapes=[
            pltpu.VMEM((2, block, quarter), bf16),
            pltpu.VMEM((2, block, quarter), bf16),
            pltpu.VMEM((block, quarter), bf16),
            pltpu.VMEM((block, quarter), bf16),
            pltpu.VMEM((EXPERTS + 8, block), f32),
            pltpu.VMEM((3, EXPERTS + 8, block), f32),
            pltpu.VMEM((places, CAP, quarter), bf16),
            pltpu.VMEM((places, 8, block), f32),
        ]
        + [dma((size,)) for size in pairs for _ in range(2)],
        compiler_params=pltpu.CompilerParams(collective_id=1, has_side_effects=True),
        cost_estimate=pl.CostEstimate(
            flops=60_000_000_000, bytes_accessed=20_000_000, transcendentals=1_000_000
        ),
    )(attended, out_all, in_part, router, pick)


def expert_kernel(
    sizes,
    rows,
    up_rows,
    weight,
    gates,
    back,
    products,
    act_low,
    pre_grads,
    returned,
    keep,
    c_out,
    c_in,
    y_out,
    y_in,
    z_out,
    p_out,
    c_send,
    c_recv,
    y_send,
    y_recv,
    z_send,
    z_recv,
    p_send,
    p_recv,
):
    bf16, f32 = jnp.bfloat16, jnp.float32
    n_fsdp, n_ctx, n_tp = sizes
    places = n_fsdp * n_ctx
    me, tp, mate, over, over_mate = around(sizes)
    width = rows.shape[2]
    quarter = width // n_tp
    hidden = weight.shape[1] // 3
    greet(
        [{"tp": mate}, {"tp": over}]
        + [place_at(sizes, later(sizes, step)) for step in range(1, places)]
    )

    def to_mate(i):
        return remote(c_out.at[i], c_in.at[i], c_send.at[i], c_recv.at[i], tp=mate)

    def to_over(i):
        return remote(y_out.at[i], y_in.at[i], y_send.at[i], y_recv.at[i], tp=over)

    def home(i):
        there = later(sizes, i + 1)
        return remote(
            z_out.at[i], back.at[me], z_send.at[i], z_recv.at[i], **place_at(sizes, there)
        )

    def home_products(i):
        there = later(sizes, i + 1)
        return remote(
            p_out.at[i], products.at[me], p_send.at[i], p_recv.at[i], **place_at(sizes, there)
        )

    def second(i):
        to_mate(i).wait_recv()
        y_out[i] = (keep[i, 0] + c_in[i, 0].astype(f32)).astype(bf16)
        to_over(i).start()

    def third(i):
        to_over(i).wait_recv()
        z_out[i] = (keep[i, 1] + c_in[i, 1].astype(f32) + y_in[i].astype(f32)).astype(bf16)

        @pl.when(i < places - 1)
        def _():
            home(i).start()

        @pl.when(i == places - 1)
        def _():
            back[me] = z_out[i]

    p_out[...] = jnp.zeros_like(p_out)

    def first(i, carry):
        there = later(sizes, i + 1)
        gate_up = dot_f32(rows[there], weight[:, : 2 * hidden], ((1,), (0,)))
        act_grads = dot_f32(up_rows[there], weight[:, 2 * hidden :], ((1,), (0,)))
        gate_part, up_part = gate_up[:, :hidden], gate_up[:, hidden:]
        slot_gates = gates[there].T[:CAP, :1]
        sigmoid = 1.0 / (1.0 + jnp.exp(-gate_part))
        silu = gate_part * sigmoid
        activated = silu * up_part
        act = (activated * slot_gates).astype(bf16)
        p_out[i, :, :CAP] = dot_f32(
            jnp.ones((8, hidden), f32), activated * act_grads, ((1,), (1,)), highest
        )
        gated = act_grads * slot_gates
        pre = jnp.concatenate(
            [gated * up_part * sigmoid * (1.0 + gate_part * (1.0 - sigmoid)), gated * silu], axis=1
        ).astype(bf16)
        act_low[there] = act
        pre_grads[there] = pre

        def input_part(which):
            return dot_f32(pre, weight[rows_at(which, quarter), : 2 * hidden], ((1,), (1,)))

        c_out[i, 0] = input_part(over_mate).astype(bf16)
        c_out[i, 1] = input_part(mate).astype(bf16)
        to_mate(i).start()
        keep[i, 0] = input_part(over)
        keep[i, 1] = input_part(tp)

        @pl.when(i < places - 1)
        def _():
            home_products(i).start()

        @pl.when(i == places - 1)
        def _():
            products[me] = p_out[i]

        @pl.when(i > 0)
        def _():
            second(i - 1)

        returned[there] = dot_f32(act, weight[:, 2 * hidden :], ((1,), (1,))).astype(bf16)

        @pl.when(i > 1)
        def _():
            third(i - 2)

        return carry

    lax.fori_loop(0, places, first, 0)
    second(places - 1)
    third(places - 2)
    third(places - 1)

    def finish(i, carry):
        to_mate(i).wait_send()
        to_over(i).wait_send()

        @pl.when(i < places - 1)
        def _():
            home(i).wait()
            home_products(i).wait()

        return carry

    lax.fori_loop(0, places, finish, 0)


def expert_stage(sizes, rows, up_rows, weight, gates):
    n_fsdp, n_ctx, n_tp = sizes
    places, _, width = rows.shape
    quarter = width // n_tp
    hidden = weight.shape[1] // 3
    bf16, f32 = jnp.bfloat16, jnp.float32
    vmem = pl.BlockSpec(memory_space=pltpu.VMEM)
    dma = pltpu.SemaphoreType.DMA
    shape = jax.ShapeDtypeStruct
    outs = (
        shape((places, CAP, quarter), bf16),
        shape(gates.shape, f32),
        shape((places, CAP, hidden), bf16),
        shape((places, CAP, 2 * hidden), bf16),
        shape((places, CAP, width), bf16),
    )
    return pl.pallas_call(
        functools.partial(expert_kernel, sizes),
        name="expert",
        out_shape=outs,
        in_specs=[vmem] * 4,
        out_specs=(vmem,) * len(outs),
        scratch_shapes=[
            pltpu.VMEM((places, 2, CAP, quarter), f32),
            pltpu.VMEM((places, 2, CAP, quarter), bf16),
            pltpu.VMEM((places, 2, CAP, quarter), bf16),
            pltpu.VMEM((places, CAP, quarter), bf16),
            pltpu.VMEM((places, CAP, quarter), bf16),
            pltpu.VMEM((places, CAP, quarter), bf16),
            pltpu.VMEM(gates.shape, f32),
        ]
        + [dma((places,)) for _ in range(8)],
        compiler_params=pltpu.CompilerParams(collective_id=2, has_side_effects=True),
        cost_estimate=pl.CostEstimate(
            flops=50_000_000_000, bytes_accessed=30_000_000, transcendentals=1_000_000
        ),
    )(rows, up_rows, weight, gates)


def back_kernel(
    sizes,
    scale,
    back,
    pick_t,
    pick,
    products,
    middle,
    small,
    chances,
    upstream,
    router,
    out_all,
    query_rot,
    key_rot,
    value,
    query_proj,
    key_proj,
    rms,
    gains,
    cosine,
    sine,
    middle_grad,
    branch_grad,
    logit_grads,
    proj_grads,
    gain_terms,
    inners,
    own_small,
    smalls,
    own_att,
    att,
    query_grad,
    key_grad,
    value_grad,
    own_sums,
    sums,
    t_send,
    t_recv,
    b_send,
    b_recv,
    z_send,
    z_recv,
    s_send,
    s_recv,
):
    bf16, f32 = jnp.bfloat16, jnp.float32
    n_fsdp, n_ctx, n_tp = sizes
    places = n_fsdp * n_ctx
    me, tp, mate, over, over_mate = around(sizes)
    ctx = lax.axis_index("ctx")
    block, quarter = middle.shape
    width = quarter * n_tp
    per = places // n_tp
    depth = quarter // per
    half_dim = HEAD_DIM // 2
    greet([in_group(sizes, step)[0] for step in range(1, n_ctx * n_tp)])

    combined = dot_f32(
        pick_t[...], back[...].reshape(EXPERTS * CAP, quarter), ((1,), (0,))
    )
    line = lax.broadcasted_iota(jnp.int32, (EXPERTS, block), 0)
    chance_grads = jnp.zeros((EXPERTS, block), f32)
    for expert in range(EXPERTS):
        found = dot_f32(
            products[expert][:, :CAP], pick[expert].astype(f32), ((1,), (0,)), highest
        )
        chance_grads = jnp.where(line == expert, found, chance_grads)
    own_small[:EXPERTS] = chance_grads
    own_small[EXPERTS:] = dot_f32(
        jnp.ones((8, quarter), f32), combined * middle[...], ((1,), (1,)), highest
    )
    total = tp_sum(own_small, smalls, t_send, t_recv, (mate, over, over_mate))
    chance = chances[...]
    chance_grads = total[:EXPERTS]
    logits = chance * (chance_grads - jnp.sum(chance * chance_grads, axis=0, keepdims=True))
    logit_grads[...] = logits
    inner = total[EXPERTS:] + jnp.sum(logits * small[:EXPERTS], axis=0, keepdims=True)
    inner = inner.T[:, :1]
    inverse = small[EXPERTS:].T[:, :1]
    for i in range(per):
        lanes = slice(i * depth, (i + 1) * depth)
        scaled = combined[:, lanes] + dot_f32(
            logits, router[tp * per + i], ((0,), (0,)), highest
        )
        middle_grad[:, lanes] = (
            upstream[:, lanes].astype(f32)
            + inverse * scaled
            - middle[:, lanes] * (inverse * inverse * inverse / width * inner)
        )
    mine, theirs = rows_at(tp, quarter), rows_at(over, quarter)
    branch_grad[:, mine] = middle_grad[...].astype(bf16)
    to_mate = remote(
        branch_grad.at[:, mine], branch_grad.at[:, mine], b_send.at[0], b_recv.at[0], tp=mate
    )
    to_over = remote(
        branch_grad.at[:, mine], branch_grad.at[:, mine], b_send.at[1], b_recv.at[1], tp=over
    )
    onward = remote(
        branch_grad.at[:, theirs], branch_grad.at[:, theirs], b_send.at[2], b_recv.at[2], tp=mate
    )
    to_over.start()
    to_mate.start()

    def from_quarter(which):
        return dot_f32(
            branch_grad[:, rows_at(which, quarter)],
            out_all[rows_at(which, quarter)],
            ((1,), (0,)),
        )

    grad = from_quarter(tp)
    to_mate.wait_recv()
    grad = grad + from_quarter(mate)
    to_over.wait_recv()
    onward.start()
    grad = grad + from_quarter(over)
    onward.wait_recv()
    grad = grad + from_quarter(over_mate)
    for copy in (to_mate, to_over, onward):
        copy.wait_send()
    to_head = {}
    for place in range(n_ctx):
        own_att[place] = grad[:, place * HEAD_DIM : (place + 1) * HEAD_DIM].astype(bf16)
        to_head[place] = remote(
            own_att.at[place], att.at[ctx], z_send.at[place], z_recv.at[ctx], ctx=place
        )

        @pl.when(ctx != place)
        def _():
            to_head[place].start()

        @pl.when(ctx == place)
        def _():
            att[ctx] = own_att[place]

    key_grad[...] = jnp.zeros_like(key_grad)
    value_grad[...] = jnp.zeros_like(value_grad)
    for place in range(n_ctx):
        here = slice(place * block, (place + 1) * block)
        seen = slice(0, (place + 1) * block)
        query = query_rot[here]
        scores = dot_f32(query, key_rot[seen], ((1,), (1,))) * scale
        exponent = jnp.exp(scores - jnp.max(scores, axis=-1, keepdims=True))
        probs = exponent / jnp.sum(exponent, axis=-1, keepdims=True)

        @pl.when(ctx != place)
        def _():
            remote(
                own_att.at[place], att.at[place], z_send.at[place], z_recv.at[place], ctx=place
            ).wait_recv()

        grad = att[place]
        prob_grads = dot_f32(grad, value[seen], ((1,), (1,)))
        score_grads = (
            probs * (prob_grads - jnp.sum(probs * prob_grads, axis=-1, keepdims=True))
        ).astype(bf16)
        query_grad[here] = dot_f32(score_grads, key_rot[seen], ((1,), (0,))) * scale
        key_grad[seen] += dot_f32(score_grads, query, ((0,), (0,))) * scale
        value_grad[seen] += dot_f32(probs.astype(bf16), grad, ((0,), (0,)))
    line = lax.broadcasted_iota(jnp.int32, own_sums.shape, 0)
    ones = jnp.ones((own_sums.shape[0], HEAD_DIM), f32)
    all_sums = jnp.zeros(own_sums.shape, f32)
    terms = [jnp.zeros((1, HEAD_DIM), f32), jnp.zeros((1, HEAD_DIM), f32)]
    for place in range(n_ctx):
        here = slice(place * block, (place + 1) * block)
        for which, grads, proj in ((0, query_grad, query_proj), (1, key_grad, key_proj)):
            turned = pltpu.roll(grads[here], half_dim, 1)
            norm_grad = grads[here] * cosine[here] - turned * sine[here]
            column = rms[:, which * n_ctx + place][:, None]
            terms[which] = terms[which] + jnp.sum(
                norm_grad * proj[here] * column, axis=0, keepdims=True
            )
            norm_grad = norm_grad * gains[which]
            grads[here] = norm_grad
            found = dot_f32(ones, norm_grad * proj[here], ((1,), (1,)), highest)
            all_sums = jnp.where(line == which * n_ctx + place, found, all_sums)
        low = value_grad[here].astype(bf16)
        proj_grads[here, 2 * HEAD_DIM :] = low
        found = dot_f32(
            ones, low.astype(f32) * value[here].astype(f32), ((1,), (1,)), highest
        )
        all_sums = jnp.where(line == 2 * n_ctx + place, found, all_sums)
    gain_terms[0] = terms[0]
    gain_terms[1] = terms[1]
    own_sums[...] = all_sums
    total = group_sum(sizes, own_sums, sums, s_send, s_recv)
    columns = total.T
    inners[...] = columns
    for place in range(n_ctx):
        here = slice(place * block, (place + 1) * block)
        for which, grads, proj in ((0, query_grad, query_proj), (1, key_grad, key_proj)):
            at = which * n_ctx + place
            column = rms[:, at][:, None]
            pre = column * grads[here] - proj[here] * (
                column * column * column / HQ * columns[:, at][:, None]
            )
            proj_grads[here, which * HEAD_DIM : (which + 1) * HEAD_DIM] = pre.astype(bf16)
    for place in range(n_ctx):

        @pl.when(ctx != place)
        def _():
            to_head[place].wait_send()


def back_stage(
    sizes,
    back,
    pick_t,
    pick,
    products,
    middle,
    small,
    chances,
    upstream,
    router,
    out_all,
    query_rot,
    key_rot,
    value,
    query_proj,
    key_proj,
    rms,
    gains,
    cosine,
    sine,
):
    n_fsdp, n_ctx, n_tp = sizes
    block, quarter = middle.shape
    length = n_ctx * block
    group = n_ctx * n_tp
    lines = 4 * n_ctx
    bf16, f32 = jnp.bfloat16, jnp.float32
    vmem = pl.BlockSpec(memory_space=pltpu.VMEM)
    dma = pltpu.SemaphoreType.DMA
    shape = jax.ShapeDtypeStruct
    outs = (
        shape((block, quarter), f32),
        shape((block, quarter * n_tp), bf16),
        shape((EXPERTS, block), f32),
        shape((length, 3 * HEAD_DIM), bf16),
        shape((2, 1, HEAD_DIM), f32),
        shape((block, lines), f32),
    )
    return pl.pallas_call(
        functools.partial(back_kernel, sizes, 1.0 / math.sqrt(HEAD_DIM)),
        name="back",
        out_shape=outs,
        in_specs=[vmem] * 19,
        out_specs=(vmem,) * len(outs),
        scratch_shapes=[
            pltpu.VMEM((EXPERTS + 8, block), f32),
            pltpu.VMEM((3, EXPERTS + 8, block), f32),
            pltpu.VMEM((n_ctx, block, HEAD_DIM), bf16),
            pltpu.VMEM((n_ctx, block, HEAD_DIM), bf16),
            pltpu.VMEM((length, HEAD_DIM), f32),
            pltpu.VMEM((length, HEAD_DIM), f32),
            pltpu.VMEM((length, HEAD_DIM), f32),
            pltpu.VMEM((lines, block), f32),
            pltpu.VMEM((group, lines, block), f32),
        ]
        + [dma((size,)) for size in (3, 3, n_ctx, group - 1) for _ in range(2)],
        compiler_params=pltpu.CompilerParams(collective_id=3, has_side_effects=True),
        cost_estimate=pl.CostEstimate(
            flops=60_000_000_000, bytes_accessed=20_000_000, transcendentals=1_000_000
        ),
    )(
        back,
        pick_t,
        pick,
        products,
        middle,
        small,
        chances,
        upstream,
        router,
        out_all,
        query_rot,
        key_rot,
        value,
        query_proj,
        key_proj,
        rms,
        gains,
        cosine,
        sine,
    )


def final_kernel(
    sizes,
    proj_grads,
    head_weight,
    normed,
    in_part,
    middle_grad,
    columns,
    grad_inputs,
    qkv_grads,
    keep,
    c_out,
    c_in,
    y_out,
    y_in,
    z_out,
    z_in,
    x_out,
    x_in,
    h_out,
    c_send,
    c_recv,
    y_send,
    y_recv,
    z_send,
    z_recv,
    x_send,
    x_recv,
    h_send,
    h_recv,
    b_send,
    b_recv,
):
    bf16, f32 = jnp.bfloat16, jnp.float32
    n_fsdp, n_ctx, n_tp = sizes
    me, tp, mate, over, over_mate = around(sizes)
    fsdp, ctx = lax.axis_index("fsdp"), lax.axis_index("ctx")
    across = 1 - fsdp
    block, quarter = in_part.shape
    width = quarter * n_tp
    depth = qkv_grads.shape[1]
    greet(
        [{"tp": mate}, {"tp": over}, {"fsdp": across}]
        + [{"ctx": lax.rem(ctx + step, n_ctx)} for step in range(1, n_ctx)]
    )

    def ahead(i):
        return lax.rem(ctx + i + 1, n_ctx)

    def to_mate(i):
        return remote(c_out.at[i], c_in.at[i], c_send.at[i], c_recv.at[i], tp=mate)

    def to_over(i):
        return remote(y_out.at[i], y_in.at[i], y_send.at[i], y_recv.at[i], tp=over)

    def home(i):
        return remote(z_out.at[i], z_in.at[i], z_send.at[i], z_recv.at[i], ctx=ahead(i))

    def to_across(i):
        return remote(x_out.at[i], x_in.at[i], x_send.at[i], x_recv.at[i], fsdp=across)

    def to_owner(i):
        return remote(h_out.at[i], qkv_grads.at[ctx], h_send.at[i], h_recv.at[i], ctx=ahead(i))

    def first(i, carry):
        grads = proj_grads[rows_at(ahead(i), block)]

        def part(which):
            return dot_f32(grads, head_weight[rows_at(which, quarter)], ((1,), (1,)))

        c_out[i, 0] = part(over_mate).astype(bf16)
        c_out[i, 1] = part(mate).astype(bf16)
        to_mate(i).start()
        keep[i, 0] = part(over)
        keep[i, 1] = part(tp)
        return carry

    def weight_part(side, i):
        lanes = rows_at(side * n_ctx + ahead(i), depth)
        total = jnp.zeros((depth, 3 * HEAD_DIM), f32)
        for place in range(n_ctx):
            total = total + dot_f32(
                normed[place, :, lanes],
                proj_grads[place * block : (place + 1) * block],
                ((0,), (0,)),
            )
        return total

    def second(i, carry):
        to_mate(i).wait_recv()
        y_out[i] = (keep[i, 0] + c_in[i, 0].astype(f32)).astype(bf16)
        to_over(i).start()
        x_out[i] = weight_part(across, i).astype(bf16)
        to_across(i).start()
        return carry

    def third(i, carry):
        to_over(i).wait_recv()
        total = keep[i, 1] + c_in[i, 1].astype(f32) + y_in[i].astype(f32)
        keep[i, 1] = total
        z_out[i] = total.astype(bf16)

        @pl.when(i < n_ctx - 1)
        def _():
            home(i).start()

        own = weight_part(fsdp, i)
        to_across(i).wait_recv()
        h_out[i] = (own + x_in[i].astype(f32)).astype(bf16)

        @pl.when(i < n_ctx - 1)
        def _():
            to_owner(i).start()

        @pl.when(i == n_ctx - 1)
        def _():
            qkv_grads[ctx] = h_out[i]

        return carry

    lax.fori_loop(0, n_ctx, first, 0)
    lax.fori_loop(0, n_ctx, second, 0)
    lax.fori_loop(0, n_ctx, third, 0)
    total = keep[n_ctx - 1, 1]
    for i in range(n_ctx - 1):
        home(i).wait_recv()
        total = total + z_in[i].astype(f32)
    first_rms, inner = columns[:, :1], columns[:, 1:2]
    grad = middle_grad[...] + first_rms * total - in_part[...] * inner
    mine, theirs = rows_at(tp, quarter), rows_at(over, quarter)
    grad_inputs[:, mine] = grad.astype(bf16)
    far = remote(
        grad_inputs.at[:, mine], grad_inputs.at[:, mine], b_send.at[0], b_recv.at[0], tp=over
    )
    near = remote(
        grad_inputs.at[:, mine], grad_inputs.at[:, mine], b_send.at[1], b_recv.at[1], tp=mate
    )
    onward = remote(
        grad_inputs.at[:, theirs], grad_inputs.at[:, theirs], b_send.at[2], b_recv.at[2], tp=mate
    )
    far.start()
    near.start()

    def finish(i, carry):
        to_mate(i).wait_send()
        to_over(i).wait_send()
        to_across(i).wait_send()

        @pl.when(i < n_ctx - 1)
        def _():
            home(i).wait_send()
            to_owner(i).wait()

        return carry

    lax.fori_loop(0, n_ctx, finish, 0)
    far.wait_recv()
    onward.start()
    near.wait()
    onward.wait()
    far.wait_send()


def final_stage(sizes, proj_grads, head_weight, normed, in_part, middle_grad, columns):
    n_fsdp, n_ctx, n_tp = sizes
    block, quarter = in_part.shape
    width = quarter * n_tp
    depth = width // (n_fsdp * n_ctx)
    bf16, f32 = jnp.bfloat16, jnp.float32
    vmem = pl.BlockSpec(memory_space=pltpu.VMEM)
    dma = pltpu.SemaphoreType.DMA
    shape = jax.ShapeDtypeStruct
    outs = (
        shape((block, width), bf16),
        shape((n_ctx, depth, 3 * HEAD_DIM), bf16),
    )
    return pl.pallas_call(
        functools.partial(final_kernel, sizes),
        name="final",
        out_shape=outs,
        in_specs=[vmem] * 6,
        out_specs=(vmem,) * len(outs),
        scratch_shapes=[
            pltpu.VMEM((n_ctx, 2, block, quarter), f32),
            pltpu.VMEM((n_ctx, 2, block, quarter), bf16),
            pltpu.VMEM((n_ctx, 2, block, quarter), bf16),
            pltpu.VMEM((n_ctx, block, quarter), bf16),
            pltpu.VMEM((n_ctx, block, quarter), bf16),
            pltpu.VMEM((n_ctx, block, quarter), bf16),
            pltpu.VMEM((n_ctx, block, quarter), bf16),
            pltpu.VMEM((n_ctx, depth, 3 * HEAD_DIM), bf16),
            pltpu.VMEM((n_ctx, depth, 3 * HEAD_DIM), bf16),
            pltpu.VMEM((n_ctx, depth, 3 * HEAD_DIM), bf16),
        ]
        + [dma((size,)) for size in (n_ctx,) * 5 + (3,) for _ in range(2)],
        compiler_params=pltpu.CompilerParams(collective_id=4, has_side_effects=True),
        cost_estimate=pl.CostEstimate(
            flops=60_000_000_000, bytes_accessed=20_000_000, transcendentals=1_000_000
        ),
    )(proj_grads, head_weight, normed, in_part, middle_grad, columns)


def by_head(
    sizes,
    inputs,
    attn_gain,
    qkv_weight,
    out_weight,
    qk_gains,
    mlp_gain,
    router_weight,
    gate_up_weight,
    down_weight,
    routes,
    cotangent,
):
    n_fsdp, n_ctx, n_tp = sizes
    places = n_fsdp * n_ctx
    both = ("fsdp", "ctx")
    f32, bf16 = jnp.float32, jnp.bfloat16
    _, block, width = inputs.shape
    depth = width // places
    quarter = width // n_tp
    length = n_ctx * block
    hidden = gate_up_weight.shape[3]
    ctx, tp = lax.axis_index("ctx"), lax.axis_index("tp")

    def own_quarter(values):
        return lax.dynamic_slice_in_dim(values, tp * quarter, quarter, axis=1)

    attn_scale = attn_gain.astype(f32)
    mlp_scale = mlp_gain.astype(f32)
    qkv_raw = qkv_weight.reshape(depth, 3, n_ctx, HEAD_DIM).transpose(2, 0, 1, 3)
    qkv_raw = qkv_raw.reshape(n_ctx, depth, 3 * HEAD_DIM).astype(f32)
    qkv_scaled = (qkv_raw * attn_scale[None, :, None]).astype(bf16)
    gate_up_raw = gate_up_weight.transpose(2, 0, 1, 3).reshape(EXPERTS, depth, 2 * hidden)
    down_raw = down_weight.transpose(1, 0, 2)
    expert_send = jnp.concatenate(
        [(gate_up_raw.astype(f32) * mlp_scale[None, :, None]).astype(bf16), down_raw], axis=2
    )
    expert_weight = lax.all_to_all(expert_send, both, 0, 0, tiled=True)
    expert_weight = expert_weight.reshape(width, 3 * hidden)
    out_all = lax.all_gather(out_weight, both, axis=0, tiled=True)
    router_f32 = router_weight.astype(f32)
    router_own = (router_f32 * mlp_scale[:, None]).T

    routed = routes.reshape(block, TOPK)
    named = (routed[:, :, None] == jnp.arange(EXPERTS, dtype=jnp.int32)).astype(f32).sum(axis=1)
    order = jnp.arange(block, dtype=jnp.int32)
    before = (order[None, :] < order[:, None]).astype(bf16)
    earlier = jnp.dot(before, named.astype(bf16), preferred_element_type=f32).astype(jnp.int32)
    slot_of = jnp.where(named > 0, earlier, -1)
    picks = slot_of.T[:, None, :] == jnp.arange(CAP, dtype=jnp.int32)[None, :, None]
    pick = picks.astype(bf16).reshape(EXPERTS * CAP, block)
    pick_t = (slot_of[:, :, None] == jnp.arange(CAP, dtype=jnp.int32)).astype(bf16)
    pick_t = pick_t.reshape(block, EXPERTS * CAP)

    def dispatch(part):
        rows = jnp.dot(pick, part, preferred_element_type=f32).astype(bf16)
        rows = lax.all_to_all(rows.reshape(EXPERTS, CAP, quarter), both, 0, 0, tiled=True)
        rows = lax.all_gather(rows, "tp", axis=2, tiled=True)
        return rows.reshape(EXPERTS * CAP, width)

    def bring_back(rows):
        rows = lax.psum_scatter(
            rows.reshape(EXPERTS, CAP, width), "tp", scatter_dimension=2, tiled=True
        )
        return combine(lax.all_to_all(rows, both, 0, 0, tiled=True))

    def combine(rows):
        rows = rows.reshape(EXPERTS * CAP, quarter)
        return lax.dot_general(pick, rows, (((0,), (0,)), ((), ())), preferred_element_type=f32)

    upstream_part = own_quarter(cotangent.reshape(block, width))
    up_rows = dispatch(upstream_part)

    flat_in = inputs.reshape(block, width).astype(f32)
    first_rms = inv_rms(flat_in)
    in_part = own_quarter(flat_in)
    normed_own = (flat_in * first_rms).astype(bf16)
    own_gains = lax.dynamic_slice_in_dim(qk_gains, ctx * HEAD_DIM, HEAD_DIM, axis=1).astype(f32)
    own_gains = own_gains[:, None, :]
    cosine, sine = signed_tables(0, length)
    (
        normed,
        head_weight,
        query_proj,
        key_proj,
        query_rot,
        key_rot,
        value_heads,
        qk_rms,
        attended,
        router_blocks,
    ) = attend(sizes, normed_own, qkv_scaled, own_gains, cosine, sine, router_own)
    head_weight = head_weight.reshape(width, 3 * HEAD_DIM)
    middle, small, chances, normed_mlp, rows, slot_gates = middle_stage(
        sizes, attended, out_all, in_part, router_blocks, pick.reshape(EXPERTS, CAP, block)
    )

    back_rows, slot_products, act_low, pre_grads, returned = expert_stage(
        sizes, rows, up_rows.reshape(places, CAP, width), expert_weight, slot_gates
    )
    rows = rows.reshape(EXPERTS * CAP, width)
    act_low = act_low.reshape(EXPERTS * CAP, hidden)
    pre_grads = pre_grads.reshape(EXPERTS * CAP, 2 * hidden)
    output_part = (middle + bring_back(returned)).astype(bf16)
    rows_in = (((0,), (0,)), ((), ()))
    expert_grads = jnp.concatenate(
        [
            lax.dot_general(rows, pre_grads, rows_in, preferred_element_type=f32),
            lax.dot_general(up_rows, act_low, rows_in, preferred_element_type=f32),
        ],
        axis=1,
    ).astype(bf16)
    expert_grads = lax.all_to_all(
        expert_grads.reshape(EXPERTS, depth, 3 * hidden), both, 0, 0, tiled=True
    ).astype(f32)

    middle_grad, branch_grad, logit_grads, proj_grads, gain_terms, inners = back_stage(
        sizes,
        back_rows,
        pick_t,
        pick.reshape(EXPERTS, CAP, block),
        slot_products,
        middle,
        small,
        chances,
        upstream_part,
        router_blocks,
        out_all,
        query_rot,
        key_rot,
        value_heads,
        query_proj,
        key_proj,
        qk_rms,
        own_gains,
        cosine,
        sine,
    )
    router_term = lax.dot_general(
        normed_mlp.astype(f32), logit_grads, (((0,), (1,)), ((), ())), precision=highest
    )
    router_term = lax.all_gather(router_term, "tp", axis=0, tiled=True)
    router_term = lax.psum_scatter(router_term, both, scatter_dimension=0, tiled=True)
    grad_router = router_term * mlp_scale[:, None]
    grad_out = lax.dot_general(branch_grad, attended, rows_in, preferred_element_type=f32)
    grad_out = lax.psum_scatter(grad_out.astype(bf16), both, scatter_dimension=0, tiled=True)
    gain_terms = lax.all_gather(
        lax.psum(gain_terms.reshape(2, HEAD_DIM), "fsdp"), "ctx", axis=1, tiled=True
    )
    own_inners = lax.dynamic_index_in_dim(inners.reshape(block, 4, n_ctx), ctx, 2, keepdims=False)
    own_rms = lax.dynamic_index_in_dim(qk_rms.reshape(block, 2, n_ctx), ctx, 2, keepdims=False)
    first_inner = epsilon * jnp.sum(own_inners[:, :2] * own_rms**3, axis=1) + own_inners[:, 2]
    columns = jnp.concatenate(
        [first_rms, first_inner[:, None] * first_rms**2 / width], axis=1
    )
    grad_inputs, qkv_grads = final_stage(
        sizes, proj_grads, head_weight, normed, in_part, middle_grad, columns
    )
    qkv_grads = qkv_grads.astype(f32)
    grad_qkv = (qkv_grads * attn_scale[None, :, None]).reshape(n_ctx, depth, 3, HEAD_DIM)
    grad_qkv = grad_qkv.transpose(1, 2, 0, 3).reshape(depth, 3, n_ctx * HEAD_DIM)
    gains = jnp.stack(
        [
            jnp.sum(qkv_grads * qkv_raw, axis=(0, 2)),
            jnp.sum(expert_grads[:, :, : 2 * hidden] * gate_up_raw.astype(f32), axis=(0, 2)),
        ]
    )
    gains = lax.psum(gains, "tp")
    grad_mlp_gain = gains[1] + jnp.sum(router_term * router_f32, axis=-1)
    output = lax.all_gather(output_part, "tp", axis=1, tiled=True)
    grad_gate_up = (expert_grads[:, :, : 2 * hidden] * mlp_scale[None, :, None]).reshape(
        EXPERTS, depth, 2, hidden
    )
    return (
        output[None],
        grad_inputs.astype(f32)[None],
        gains[0],
        grad_qkv,
        grad_out.astype(f32),
        gain_terms,
        grad_mlp_gain,
        grad_router,
        grad_gate_up.transpose(1, 2, 0, 3),
        expert_grads[:, :, 2 * hidden :].transpose(1, 0, 2),
    )


def solution(mesh):
    sizes = (mesh.shape["fsdp"], mesh.shape["ctx"], mesh.shape["tp"])
    one_expert = sizes[0] * sizes[1] == EXPERTS
    one_head = sizes[1] * sizes[2] * HEAD_DIM == HQ

    def step(*arrays):
        if one_expert and one_head and arrays[0].shape[0] == 1:
            return by_head(sizes, *arrays)
        return on_device(*arrays)

    placed = (
        P("fsdp", "ctx", None),
        P(("fsdp", "ctx")),
        P(("fsdp", "ctx"), None, "tp"),
        P(("fsdp", "ctx"), "tp"),
        P(None, "tp"),
        P(("fsdp", "ctx")),
        P(("fsdp", "ctx"), None),
        P(("fsdp", "ctx"), None, None, "tp"),
        P(("fsdp", "ctx"), None, "tp"),
        P("ctx", "fsdp", None, None),
        P("fsdp", "ctx", None),
    )
    return jax.shard_map(
        step,
        mesh=mesh,
        in_specs=placed,
        out_specs=(
            P("fsdp", "ctx", None),
            P("fsdp", "ctx", None),
            P(("fsdp", "ctx")),
            P(("fsdp", "ctx"), None, "tp"),
            P(("fsdp", "ctx"), "tp"),
            P(None, "tp"),
            P(("fsdp", "ctx")),
            P(("fsdp", "ctx"), None),
            P(("fsdp", "ctx"), None, None, "tp"),
            P(("fsdp", "ctx"), None, "tp"),
        ),
        check_vma=False,
    )
```
